128 devices in a mesh: dp: 16 (over y, z), tensor: 8 (over x, core).
Axes of the slice: x: 4, y: 4, z: 4, core: 2. Of those that a mesh axis runs over, the one named last changes fastest.
Arguments:
- prefill_rows: bfloat16 [8192, 2048], P(('dp', 'tensor')), may hold values from -6 to 6
- decode_rows: bfloat16 [256, 2048], P(('dp', 'tensor')), may hold values from -6 to 6
- deal_order: int32 [256], replicated, may hold values from 0 to 255, each once
- prefill_offset: int32 [16], P('dp'), may hold values from 0 to 1024, as said below
- cache_length: int32 [256], P('dp'), may hold values from 1 to 1024, as said below
- prefill_cache: bfloat16 [2, 16, 1024, 1024], P(None, 'dp', None, 'tensor'), may hold values from -480 to 480, as said below
- decode_cache: bfloat16 [2, 256, 1024, 1024], P(None, 'dp', None, 'tensor'), may hold values from -480 to 480, as said below
- qkv_weight: bfloat16 [2048, 8, 512], P(None, 'tensor'), may hold values from -0.125 to 0.125
- out_weight: bfloat16 [2048, 2048], P('tensor'), may hold values from -0.125 to 0.125
- attention_gain: float32 [2048], replicated, may hold values from 0.1 to 1.9
- forward_gain: float32 [2048], replicated, may hold values from 0.1 to 1.9
- gate_weight: bfloat16 [2048, 8192], P(None, 'tensor'), may hold values from -0.125 to 0.125
- up_weight: bfloat16 [2048, 8192], P(None, 'tensor'), may hold values from -0.125 to 0.125
- down_weight: bfloat16 [8192, 2048], P('tensor'), may hold values from -0.0625 to 0.0625
Outputs:
- prefill_out: bfloat16 [8192, 2048], P(('dp', 'tensor'))
- decode_out: bfloat16 [256, 2048], P(('dp', 'tensor'))
- prefill_entries: bfloat16 [2, 8192, 1024], P(None, 'dp', 'tensor')
- decode_entries: bfloat16 [2, 256, 1024], P(None, 'dp', 'tensor')
The draws below stay inside these ranges and needn't reach their ends.
Inputs may be any that keep to these rules, and one draw needn't show every extreme that they name: A permutation: request r is held in slot deal_order[r]; slot s belongs to request group s // 16. `prefill_offset`: stored positions of each prefill request; some request has exactly 1024. `cache_length`: stored positions of the decode request in each slot; some slot has exactly 1024. `prefill_cache`: stored rotated keys and values; positions at or past a request's stored count hold unrelated numbers. `decode_cache`: stored rotated keys and values; positions at or past a slot's stored count hold unrelated numbers.
All inputs are finite; a program needn't handle non-finite values.
Results may differ from the reference program's by a relative error of at most 0.015.
The reference program's roundings to bfloat16 on the way count: a program that leaves them out, or rounds other values in their place, can miss the bound.
Values may be sent and summed in bfloat16 or wider, within the bound.
A program may use at most 128 MiB of HBM per device.

```python
import jax
import jax.numpy as jnp
from jax import lax

D = 2048
H = 16
KVH = 8
HD = 128
FF = 8192
PTOK = 512
PCACHE = 1024
CACHE = 1024
RDT = 2
NDEC = 256
NPRE = 16
N_DP = 16
N_TENSOR = 8


def cache_draw(key, entries, stored):
    noise = jax.random.normal(key, (2, entries, stored, KVH * HD), jnp.float32)
    noise = jnp.clip(noise, -6.0, 6.0)
    return noise


def draw_prefill_cache(key, part):
    return cache_draw(key, NPRE, PCACHE).astype(jnp.bfloat16)


def draw_decode_cache(key, part):
    return cache_draw(key, NDEC, CACHE).astype(jnp.bfloat16)


def draw_cache_length(key, part):
    first = jax.random.randint(jax.random.fold_in(key, 1), (NDEC,), 1, CACHE + 1)
    second = jax.random.randint(jax.random.fold_in(key, 2), (NDEC,), 1, CACHE + 1)
    lengths = jnp.minimum(first, second).astype(jnp.int32)
    pinned = jax.random.randint(jax.random.fold_in(key, 3), (), 0, NDEC)
    return lengths.at[pinned].set(CACHE)


def draw_prefill_offset(key, part):
    offsets = jax.random.randint(jax.random.fold_in(key, 4), (NPRE,), 0, PCACHE + 1).astype(jnp.int32)
    pinned = jax.random.randint(jax.random.fold_in(key, 5), (), 0, NPRE)
    return offsets.at[pinned].set(PCACHE)


def block_scale(stream_key, shape, cuts, least, largest):
    level = 1.0
    for dim, parts in cuts:
        steps = jax.random.uniform(jax.random.fold_in(jax.random.fold_in(stream_key, 6), dim), (parts,), jnp.float32, least / len(cuts), largest / len(cuts))
        level = level * jnp.repeat(jnp.exp(steps), shape[dim] // parts).reshape((-1,) + (1,) * (len(shape) - 1 - dim))
    return level


def bell_draw(key, shape, deviation, most, split=(), held_as=jnp.bfloat16):
    level = block_scale(key, shape, split, -0.22, 0.18) if split else 1.0
    drawn = jax.random.normal(key, shape, jnp.float32) * deviation * level
    return jnp.minimum(jnp.maximum(drawn, -most), most).astype(held_as)


def setup_inputs(seed: int = 0) -> dict:
    streams_of = jax.random.split(jax.random.key(seed), 15)
    prefill_rows = bell_draw(streams_of[0], (NPRE * PTOK, D), 1.0, 6.0, ((0, 128),))
    decode_rows = bell_draw(streams_of[1], (NDEC, D), 1.0, 6.0, ((0, 128),))
    deal_order = jax.random.permutation(streams_of[2], NDEC).astype(jnp.int32)
    prefill_offset = draw_prefill_offset(jax.random.fold_in(streams_of[14], 71), 0)
    cache_length = draw_cache_length(jax.random.fold_in(streams_of[14], 71), 0)
    prefill_cache = draw_prefill_cache(jax.random.fold_in(streams_of[14], 71), 0)
    decode_cache = draw_decode_cache(jax.random.fold_in(streams_of[14], 71), 0)
    qkv_weight = bell_draw(streams_of[7], (D, KVH, (H // KVH + 2) * HD), D ** -0.5, 0.125, ((1, 8),))
    out_weight = bell_draw(streams_of[8], (H * HD, D), (H * HD) ** -0.5, 0.125, ((0, 8),))
    attention_gain = jnp.clip(1.0 + 0.18 * jax.random.normal(streams_of[9], (D,), jnp.float32), 0.1, 1.9)
    forward_gain = jnp.clip(1.0 + 0.18 * jax.random.normal(streams_of[10], (D,), jnp.float32), 0.1, 1.9)
    gate_weight = bell_draw(streams_of[11], (D, FF), D ** -0.5, 0.125, ((1, 8),))
    up_weight = bell_draw(streams_of[12], (D, FF), D ** -0.5, 0.125, ((1, 8),))
    down_weight = bell_draw(streams_of[13], (FF, D), FF ** -0.5, 0.0625, ((0, 8),))
    return dict(prefill_rows=prefill_rows, decode_rows=decode_rows, deal_order=deal_order, prefill_offset=prefill_offset, cache_length=cache_length, prefill_cache=prefill_cache, decode_cache=decode_cache, qkv_weight=qkv_weight, out_weight=out_weight, attention_gain=attention_gain, forward_gain=forward_gain, gate_weight=gate_weight, up_weight=up_weight, down_weight=down_weight)


EPSILON = 1e-06
THETA = 1000000.0
NEGATIVE = -1e+30

def root_norm(rows, gain):
    values = rows.astype(jnp.float32)
    spread = lax.optimization_barrier(jnp.mean(values * values, axis=-1, keepdims=True))
    return (values * lax.rsqrt(spread + EPSILON) * gain.astype(jnp.float32)).astype(jnp.bfloat16)

def rotate(vectors, places):
    halfway = vectors.shape[-1] // 2
    powers = jnp.arange(halfway, dtype=jnp.float32) * (2.0 / vectors.shape[-1])
    inverse = THETA ** (-powers)
    angles = places.astype(jnp.float32)[:, None] * inverse[None, :]
    cosine = jnp.cos(angles)[:, None, :]
    sine_part = jnp.sin(angles)[:, None, :]
    leading = vectors[..., :halfway]
    trailing = vectors[..., halfway:]
    return jnp.concatenate([leading * cosine - trailing * sine_part, trailing * cosine + leading * sine_part], axis=-1)

def project(normed, places, qkv_weight):
    heads = qkv_weight.shape[1]
    width = qkv_weight.shape[2]
    groups = width // HD - 2
    count = normed.shape[0]
    mixed = jnp.dot(normed, qkv_weight.reshape(qkv_weight.shape[0], heads * width), preferred_element_type=jnp.float32)
    mixed = mixed.reshape(count, heads, groups + 2, HD)
    queries = rotate(mixed[:, :, :groups].reshape(count, heads * groups, HD), places)
    queries = queries.reshape(count, heads, groups, HD).astype(jnp.bfloat16)
    new_keys = rotate(mixed[:, :, groups], places).astype(jnp.bfloat16)
    new_values = mixed[:, :, groups + 1].astype(jnp.bfloat16)
    return (queries, new_keys, new_values)

def fill_attend(queries, new_keys, new_values, cache_keys, cache_values, offset):
    scaling = 1.0 / HD ** 0.5
    count = queries.shape[0]
    prior_count = cache_keys.shape[0]
    query_wide = queries.astype(jnp.float32)
    cached_scores = jnp.einsum('qkgd,skd->kgqs', query_wide, cache_keys.astype(jnp.float32)) * scaling
    fresh_scores = jnp.einsum('qkgd,skd->kgqs', query_wide, new_keys.astype(jnp.float32)) * scaling
    cached_allowed = jnp.arange(prior_count, dtype=jnp.int32)[None, :] < offset
    fresh_allowed = jnp.arange(count, dtype=jnp.int32)[None, :] <= jnp.arange(count, dtype=jnp.int32)[:, None]
    scores = jnp.concatenate([jnp.where(cached_allowed, cached_scores, NEGATIVE), jnp.where(fresh_allowed, fresh_scores, NEGATIVE)], axis=-1)
    row_top = lax.optimization_barrier(jnp.max(scores, axis=-1, keepdims=True))
    weights = jnp.exp(scores - row_top)
    weights = (weights / lax.optimization_barrier(jnp.sum(weights, axis=-1, keepdims=True))).astype(jnp.bfloat16).astype(jnp.float32)
    attended = jnp.einsum('kgqs,skd->qkgd', weights[..., :prior_count], cache_values.astype(jnp.float32))
    attended = attended + jnp.einsum('kgqs,skd->qkgd', weights[..., prior_count:], new_values.astype(jnp.float32))
    return attended.astype(jnp.bfloat16)

def step_attend(queries, new_keys, new_values, cache_keys, cache_values, lengths):
    scaling = 1.0 / HD ** 0.5
    stored = cache_keys.shape[1]
    query_wide = queries.astype(jnp.float32)
    cached_scores = jnp.einsum('nkgd,nskd->nkgs', query_wide, cache_keys.astype(jnp.float32)) * scaling
    own_scores = jnp.einsum('nkgd,nkd->nkg', query_wide, new_keys.astype(jnp.float32))[..., None] * scaling
    allowed = (jnp.arange(stored, dtype=jnp.int32)[None, :] < lengths[:, None])[:, None, None, :]
    scores = jnp.concatenate([jnp.where(allowed, cached_scores, NEGATIVE), own_scores], axis=-1)
    row_top = lax.optimization_barrier(jnp.max(scores, axis=-1, keepdims=True))
    weights = jnp.exp(scores - row_top)
    weights = (weights / lax.optimization_barrier(jnp.sum(weights, axis=-1, keepdims=True))).astype(jnp.bfloat16).astype(jnp.float32)
    attended = jnp.einsum('nkgs,nskd->nkgd', weights[..., :stored], cache_values.astype(jnp.float32))
    attended = attended + weights[..., stored:] * new_values.astype(jnp.float32)[:, :, None, :]
    return attended.astype(jnp.bfloat16)

def feed_forward(inner, gate_weight, up_weight, down_weight):
    gate_part = jnp.dot(inner, gate_weight, preferred_element_type=jnp.float32)
    up_part = jnp.dot(inner, up_weight, preferred_element_type=jnp.float32)
    hidden = (jax.nn.silu(gate_part) * up_part).astype(jnp.bfloat16)
    return jnp.dot(hidden, down_weight, preferred_element_type=jnp.float32)

def reference(prefill_rows, decode_rows, deal_order, prefill_offset, cache_length, prefill_cache, decode_cache, qkv_weight, out_weight, attention_gain, forward_gain, gate_weight, up_weight, down_weight):
    groups = H // KVH
    holder = jnp.zeros((NDEC,), jnp.int32).at[deal_order].set(jnp.arange(NDEC, dtype=jnp.int32))
    dealt = decode_rows[holder]
    fill_normed = root_norm(prefill_rows, attention_gain)
    step_normed = root_norm(dealt, attention_gain)
    fill_places = (prefill_offset[:, None] + jnp.arange(PTOK, dtype=jnp.int32)[None, :]).reshape(NPRE * PTOK)
    fill_query, fill_keys, fill_values = project(fill_normed, fill_places, qkv_weight)
    step_query, step_keys, step_values = project(step_normed, cache_length, qkv_weight)

    def one_request(members):
        return fill_attend(*members)
    fill_att = lax.map(one_request, (fill_query.reshape(NPRE, PTOK, KVH, groups, HD), fill_keys.reshape(NPRE, PTOK, KVH, HD), fill_values.reshape(NPRE, PTOK, KVH, HD), prefill_cache[0].reshape(NPRE, PCACHE, KVH, HD), prefill_cache[1].reshape(NPRE, PCACHE, KVH, HD), prefill_offset))
    fill_att = fill_att.reshape(NPRE * PTOK, H * HD)

    def one_group(members):
        return step_attend(*members)
    slot_group = RDT * N_TENSOR
    step_att = lax.map(one_group, (step_query.reshape(N_DP, slot_group, KVH, groups, HD), step_keys.reshape(N_DP, slot_group, KVH, HD), step_values.reshape(N_DP, slot_group, KVH, HD), decode_cache[0].reshape(N_DP, slot_group, CACHE, KVH, HD), decode_cache[1].reshape(N_DP, slot_group, CACHE, KVH, HD), cache_length.reshape(N_DP, slot_group)))
    step_att = step_att.reshape(NDEC, H * HD)
    fill_resid = (prefill_rows.astype(jnp.float32) + jnp.dot(fill_att, out_weight, preferred_element_type=jnp.float32)).astype(jnp.bfloat16)
    step_resid = (dealt.astype(jnp.float32) + jnp.dot(step_att, out_weight, preferred_element_type=jnp.float32)).astype(jnp.bfloat16)
    fill_final = (fill_resid.astype(jnp.float32) + feed_forward(root_norm(fill_resid, forward_gain), gate_weight, up_weight, down_weight)).astype(jnp.bfloat16)
    step_final = (step_resid.astype(jnp.float32) + feed_forward(root_norm(step_resid, forward_gain), gate_weight, up_weight, down_weight)).astype(jnp.bfloat16)
    decode_out = step_final[deal_order]
    prefill_entries = jnp.stack([fill_keys.reshape(NPRE * PTOK, KVH * HD), fill_values.reshape(NPRE * PTOK, KVH * HD)])
    decode_entries = jnp.stack([step_keys.reshape(NDEC, KVH * HD), step_values.reshape(NDEC, KVH * HD)])
    return (fill_final, decode_out, prefill_entries, decode_entries)
```

```python
import functools
import math

import jax
import jax.numpy as jnp
from jax import lax
from jax.experimental import pallas as pl
from jax.experimental.pallas import tpu as pltpu
from jax.sharding import PartitionSpec as P

HD = 128
EPSILON = 1e-06
THETA = 1000000.0
NEGATIVE = -1e30
MESH = pl.DeviceIdType.MESH
F32 = jnp.float32
BF16 = jnp.bfloat16
NT = (((1,), (1,)), ((), ()))
HALF = 32
CHUNKS = 4


def normed(values, gain):
    spread = jnp.mean(values * values, axis=-1, keepdims=True)
    return (values * lax.rsqrt(spread + EPSILON) * gain).astype(BF16)


def layer_kernel(
    groups,
    rows_ref,
    drows_ref,
    deal_ref,
    off_ref,
    len_ref,
    cos_ref,
    sin_ref,
    again_ref,
    fgain_ref,
    pcache,
    dcache,
    qkv_hbm,
    out_hbm,
    gate_hbm,
    up_hbm,
    down_hbm,
    pout_ref,
    dout_ref,
    pent_ref,
    dent_ref,
    w_qkv,
    w_out,
    w_gate,
    w_up,
    w_down,
    kall,
    vall,
    kdec,
    vdec,
    xg1,
    xg2,
    mixed,
    qb,
    att,
    pb,
    rcv,
    cb,
    fb,
    nb,
    resid,
    hid,
    dpart,
    drs,
    dpb,
    dag,
    dsc,
    dpr,
    qpad,
    knew,
    vnew,
    dob,
    wsem,
    ags,
    agr,
    rss,
    rsr,
    crs,
    crr,
    dps,
    dpr_sem,
    cas,
    car,
):
    g = lax.axis_index("dp")
    t = lax.axis_index("tensor")
    x = t // 2
    c = t % 2
    width = rows_ref.shape[1]
    cw = width // CHUNKS
    bw = width // 8
    stored = pcache.shape[2]
    fresh = pent_ref.shape[1]
    slots = dent_ref.shape[1]
    dstored = dcache.shape[2]
    units = w_gate.shape[1]
    nreq = groups * slots
    scale2 = (1.0 / math.sqrt(HD)) * math.log2(math.e)

    partner = (g, t + 1 - 2 * c)
    right = (g, ((x + 1) % 4) * 2 + c)
    left = (g, ((x + 3) % 4) * 2 + c)
    sends = []

    def remote(src, dst, ss, rs, dev):
        copy = pltpu.make_async_remote_copy(
            src_ref=src, dst_ref=dst, send_sem=ss, recv_sem=rs, device_id=dev, device_id_type=MESH
        )
        copy.start()
        sends.append(copy)

    def arrived(dst, ss, rs):
        pltpu.make_async_remote_copy(
            src_ref=dst, dst_ref=dst, send_sem=ss, recv_sem=rs, device_id=partner, device_id_type=MESH
        ).wait_recv()

    local = {}

    def fetch(name, index, src, dst):
        copy = pltpu.make_async_copy(src, dst, wsem.at[index])
        copy.start()
        local[name] = copy

    fetch("qkv", 0, qkv_hbm, w_qkv)
    fetch("pk", 1, pcache.at[0, 0], kall.at[pl.ds(0, stored)])
    fetch("pv", 2, pcache.at[1, 0], vall.at[pl.ds(0, stored)])
    fetch("out", 3, out_hbm, w_out)
    fetch("dk", 4, dcache.at[0], kdec)
    fetch("dv", 5, dcache.at[1], vdec)
    fetch("gate", 6, gate_hbm, w_gate)
    fetch("up", 7, up_hbm, w_up)
    fetch("down", 8, down_hbm, w_down)

    barrier = pltpu.get_barrier_semaphore()
    for k in range(1, 8):
        pl.semaphore_signal(barrier, inc=1, device_id=(g, (t + k) % 8), device_id_type=MESH)
    for k in range(1, groups):
        pl.semaphore_signal(barrier, inc=1, device_id=((g + k) % groups, t), device_id_type=MESH)

    def buffer_of(stage, h):
        return (xg1 if stage == 0 else xg2).at[h]

    def ag_block(stage, h, b, p):
        return buffer_of(stage, h).at[pl.ds(HALF * b + 16 * p, 16)]

    def ag_send(stage, h, src_b, dst_b, p, number, dev):
        remote(
            ag_block(stage, h, src_b, p),
            ag_block(stage, h, dst_b, p),
            ags.at[stage, h, number],
            agr.at[stage, h, number],
            dev,
        )

    def ag_wait(stage, h, b, p, number):
        arrived(ag_block(stage, h, b, p), ags.at[stage, h, number], agr.at[stage, h, number])

    def ag_start(stage, h):
        ag_send(stage, h, 0, 6, 0, 1, right)
        ag_send(stage, h, 0, 2, 1, 4, left)
        ag_send(stage, h, 0, 6, 1, 2, right)
        ag_send(stage, h, 0, 2, 0, 3, left)
        ag_send(stage, h, 0, 1, 0, 0, partner)
        ag_send(stage, h, 0, 1, 1, 13, partner)

    def ag_forward(stage, h):
        ag_wait(stage, h, 6, 0, 1)
        ag_send(stage, h, 6, 4, 0, 5, right)
        ag_wait(stage, h, 2, 1, 4)
        ag_send(stage, h, 2, 4, 1, 6, left)
        ag_send(stage, h, 6, 7, 0, 7, partner)
        ag_send(stage, h, 2, 3, 1, 10, partner)
        ag_wait(stage, h, 6, 1, 2)
        ag_send(stage, h, 6, 7, 1, 8, partner)
        ag_wait(stage, h, 2, 0, 3)
        ag_send(stage, h, 2, 3, 0, 9, partner)

    def ag_far(stage, h):
        ag_wait(stage, h, 4, 0, 5)
        ag_send(stage, h, 4, 5, 0, 11, partner)
        ag_wait(stage, h, 4, 1, 6)
        ag_send(stage, h, 4, 5, 1, 12, partner)

    def ag_finish(stage, h):
        for b, p, number in (
            (1, 0, 0),
            (1, 1, 13),
            (7, 0, 7),
            (3, 1, 10),
            (7, 1, 8),
            (3, 0, 9),
            (5, 0, 11),
            (5, 1, 12),
        ):
            ag_wait(stage, h, b, p, number)

    def rs_split(stage, h, n, part):
        for b in range(8):
            pb[stage, h, n, b % 2, b // 2] = part[HALF * b : HALF * (b + 1)].astype(BF16)
        remote(
            pb.at[stage, h, n, 1],
            rcv.at[stage, h, n],
            rss.at[stage, h, n, 0],
            rsr.at[stage, h, n, 0],
            partner,
        )

    def on_chip(stage, h, n, d):
        return pb[stage, h, n, 0, d].astype(F32) + rcv[stage, h, n, d].astype(F32)

    def to_side(stage, h, n, d):
        side, dev = (0, right) if d == 1 else (1, left)
        remote(
            cb.at[stage, h, n, d],
            nb.at[stage, h, n, side],
            rss.at[stage, h, n, 2 + side],
            rsr.at[stage, h, n, 2 + side],
            dev,
        )

    def rs_combine(stage, h, n):
        arrived(rcv.at[stage, h, n], rss.at[stage, h, n, 0], rsr.at[stage, h, n, 0])
        cb[stage, h, n, 2] = on_chip(stage, h, n, 2).astype(BF16)
        remote(
            cb.at[stage, h, n, 2],
            fb.at[stage, h, n],
            rss.at[stage, h, n, 1],
            rsr.at[stage, h, n, 1],
            right if n % 2 == 0 else left,
        )
        d = 3 if n % 2 == 0 else 1
        cb[stage, h, n, d] = on_chip(stage, h, n, d).astype(BF16)
        to_side(stage, h, n, d)

    def rs_relay(stage, h, n):
        arrived(fb.at[stage, h, n], rss.at[stage, h, n, 1], rsr.at[stage, h, n, 1])
        d = 1 if n % 2 == 0 else 3
        cb[stage, h, n, d] = (on_chip(stage, h, n, d) + fb[stage, h, n].astype(F32)).astype(BF16)
        to_side(stage, h, n, d)

    def rs_total(stage, h, n):
        for side in range(2):
            arrived(
                nb.at[stage, h, n, side],
                rss.at[stage, h, n, 2 + side],
                rsr.at[stage, h, n, 2 + side],
            )
        return (
            on_chip(stage, h, n, 0) + nb[stage, h, n, 0].astype(F32) + nb[stage, h, n, 1].astype(F32)
        )

    def columns(p):
        return pl.ds(pl.multiple_of(p * bw, bw), bw)

    def cr_start(i):
        for k in range(1, 8):
            p = (t + k) % 8
            remote(
                dpart.at[i, :, columns(p)], drs.at[i, k], crs.at[i, k], crr.at[i, k], (g, p)
            )

    def cr_total(i):
        total = dpart[i, :, columns(t)].astype(F32)
        for k in range(1, 8):
            arrived(drs.at[i, k], crs.at[i, k], crr.at[i, k])
            total = total + drs[i, k].astype(F32)
        return total

    def dp_start(i, block):
        dpb[i, g] = block
        for k in range(1, groups):
            remote(
                dpb.at[i, g], dpb.at[i, g], dps.at[i, k], dpr_sem.at[i, k], ((g + k) % groups, t)
            )

    def dp_total(i):
        for k in range(1, groups):
            source = (g + groups - k) % groups
            arrived(dpb.at[i, source], dps.at[i, k], dpr_sem.at[i, k])
        return dpb[i].reshape(nreq, bw)

    def ca_start(i, block):
        dag[i, :, columns(t)] = block
        for k in range(1, 8):
            mine = dag.at[i, :, columns(t)]
            remote(mine, mine, cas.at[i, k], car.at[i, k], (g, (t + k) % 8))

    def ca_finish(i):
        for k in range(1, 8):
            arrived(dag.at[i, :, columns((t + 8 - k) % 8)], cas.at[i, k], car.at[i, k])

    def rotated(part, cosine, sine):
        return part * cosine + pltpu.roll(part, HD // 2, 1) * sine

    def project(h):
        mixed[...] = jnp.dot(xg1[h], w_qkv[...], preferred_element_type=F32)

        def one(b, carry):
            owner = 2 * ((x + b // 2) % 4) + (c + b % 2) % 2
            first = pl.multiple_of(owner * (2 * HALF) + HALF * h, HALF)
            place = pl.ds(first, HALF)
            here = pl.ds(pl.multiple_of(HALF * b, HALF), HALF)
            cosine = cos_ref[place, :]
            sine = sin_ref[place, :]
            for head in range(2):
                qb[h, head, here, :] = rotated(
                    mixed[here, HD * head : HD * (head + 1)], cosine, sine
                ).astype(BF16)
            key = rotated(mixed[here, 2 * HD : 3 * HD], cosine, sine).astype(BF16)
            value = mixed[here, 3 * HD : 4 * HD].astype(BF16)
            cached = pl.ds(pl.multiple_of(stored + first, HALF), HALF)
            kall[cached, :] = key
            vall[cached, :] = value
            pent_ref[0, place, :] = key
            pent_ref[1, place, :] = value
            return carry

        lax.fori_loop(0, 8, one, 0)

    def attend(h, i):
        rows = 4 * HALF
        here = pl.ds(rows * i, rows)
        query = jnp.concatenate([qb[h, 0, here, :], qb[h, 1, here, :]], axis=0)
        scores = lax.dot_general(query, kall[...], NT, preferred_element_type=F32)
        r = lax.broadcasted_iota(jnp.int32, (2 * rows, 1), 0)
        b = 4 * i + ((r >> 5) & 3)
        owner = 2 * ((x + (b >> 1)) & 3) + ((c + (b & 1)) & 1)
        q_place = owner * (2 * HALF) + HALF * h + (r & 31)
        col = lax.broadcasted_iota(jnp.int32, (1, stored + fresh), 1)
        k_place = jnp.where(
            col < stored, jnp.where(col < off_ref[0], -1, stored + fresh), col - stored
        )
        scores = jnp.where(k_place <= q_place, scores, NEGATIVE)
        top = jnp.max(scores, axis=-1, keepdims=True)
        weights = jnp.exp2((scores - top) * scale2)
        total = jnp.sum(weights, axis=-1, keepdims=True)
        result = jnp.dot(weights.astype(BF16), vall[...], preferred_element_type=F32)
        result = (result / total).astype(BF16)
        att[h, here, 0:HD] = result[:rows]
        att[h, here, HD : 2 * HD] = result[rows:]

    def out_project(h):
        for n in range(CHUNKS):
            part = jnp.dot(
                att[h], w_out[:, cw * n : cw * (n + 1)], preferred_element_type=F32
            )
            rs_split(0, h, n, part)

    def middle(h):
        mine = pl.ds(HALF * h, HALF)
        pieces = []
        for n in range(CHUNKS):
            cols = slice(cw * n, cw * (n + 1))
            value = (rows_ref[mine, cols].astype(F32) + rs_total(0, h, n)).astype(BF16)
            resid[mine, cols] = value
            pieces.append(value.astype(F32))
        values = jnp.concatenate(pieces, axis=1)
        xg2[h, 0:HALF, :] = normed(values, fgain_ref[...])
        ag_start(1, h)

    def gated(h):
        count = 8 * HALF + (slots if h == 0 else 0)
        step = 256

        def one(j, carry):
            cols = pl.ds(pl.multiple_of(j * step, step), step)
            inner = xg2[h, 0:count, :]
            gate_part = jnp.dot(inner, w_gate[:, cols], preferred_element_type=F32)
            up_part = jnp.dot(inner, w_up[:, cols], preferred_element_type=F32)
            hid[h, 0:count, cols] = (
                gate_part / (1.0 + jnp.exp(-gate_part)) * up_part
            ).astype(BF16)
            return carry

        lax.fori_loop(0, units // step, one, 0)

    def lower(h):
        count = 8 * HALF + (slots if h == 0 else 0)
        for n in range(CHUNKS):
            cols = slice(cw * n, cw * (n + 1))
            part = jnp.dot(hid[h, 0:count, :], w_down[:, cols], preferred_element_type=F32)
            rs_split(1, h, n, part)
            if h == 0:
                dpart[2, :, cols] = part[8 * HALF :].astype(BF16)

    def last(h):
        mine = pl.ds(HALF * h, HALF)
        for n in range(CHUNKS):
            cols = slice(cw * n, cw * (n + 1))
            pout_ref[mine, cols] = (resid[mine, cols].astype(F32) + rs_total(1, h, n)).astype(BF16)

    wide = 16 * slots

    def marker(head, flip):
        shape = (slots, wide) if flip else (wide, slots)
        row = lax.broadcasted_iota(jnp.int32, shape, 1 if flip else 0)
        slot = lax.broadcasted_iota(jnp.int32, shape, 0 if flip else 1)
        return (row == 16 * slot + head).astype(F32).astype(BF16)

    def decode_project():
        inner = normed(dag[0].astype(F32), again_ref[...])
        part = jnp.dot(inner, w_qkv[...], preferred_element_type=F32)
        cosine = cos_ref[fresh : fresh + slots, :]
        sine = sin_ref[fresh : fresh + slots, :]
        spread = jnp.zeros((wide, HD), F32)
        for head in range(2):
            query = rotated(part[:, HD * head : HD * (head + 1)], cosine, sine).astype(BF16)
            spread = spread + jnp.dot(marker(head, False), query, preferred_element_type=F32)
        qpad[...] = spread.astype(BF16)
        key = rotated(part[:, 2 * HD : 3 * HD], cosine, sine).astype(BF16)
        value = part[:, 3 * HD : 4 * HD].astype(BF16)
        dent_ref[0] = key
        dent_ref[1] = value
        knew[...] = jnp.zeros_like(knew)
        vnew[...] = jnp.zeros_like(vnew)
        knew[0:slots, :] = key
        vnew[0:slots, :] = value

    def decode_attend():
        def score(n, carry):
            here = pl.ds(pl.multiple_of(16 * n, 16), 16)
            part = lax.dot_general(qpad[here, :], kdec[n], NT, preferred_element_type=F32)
            col = lax.broadcasted_iota(jnp.int32, (16, dstored), 1)
            dsc[here, 0:dstored] = jnp.where(col < len_ref[n], part, NEGATIVE)
            return carry

        lax.fori_loop(0, slots, score, 0, unroll=4)
        own = lax.dot_general(qpad[...], knew[...], NT, preferred_element_type=F32)
        row = lax.broadcasted_iota(jnp.int32, (wide, HD), 0)
        col = lax.broadcasted_iota(jnp.int32, (wide, HD), 1)
        dsc[:, dstored:] = jnp.where(col == (row >> 4), own, NEGATIVE)
        scores = dsc[...]
        top = jnp.max(scores, axis=-1, keepdims=True)
        weights = jnp.exp2((scores - top) * scale2)
        total = jnp.sum(weights, axis=-1, keepdims=True)
        dpr[...] = weights.astype(BF16)

        def mix(n, carry):
            here = pl.ds(pl.multiple_of(16 * n, 16), 16)
            dob[here, :] = jnp.dot(dpr[here, 0:dstored], vdec[n], preferred_element_type=F32)
            return carry

        lax.fori_loop(0, slots, mix, 0, unroll=4)
        result = dob[...] + jnp.dot(dpr[:, dstored:], vnew[...], preferred_element_type=F32)
        result = (result / total).astype(BF16)
        picked = [
            jnp.dot(marker(head, True), result, preferred_element_type=F32).astype(BF16)
            for head in range(2)
        ]
        attended = jnp.concatenate(picked, axis=1)
        dpart[1] = jnp.dot(attended, w_out[...], preferred_element_type=F32).astype(BF16)

    for h in range(2):
        mine = pl.ds(HALF * h, HALF)
        xg1[h, 0:HALF, :] = normed(rows_ref[mine, :].astype(F32), again_ref[...])
    pair = drows_ref[...].astype(F32)
    spot = lax.broadcasted_iota(jnp.int32, (slots, width), 0)
    dpart[0] = (
        jnp.where(spot == 2 * t, pair[0:1], 0.0) + jnp.where(spot == 2 * t + 1, pair[1:2], 0.0)
    ).astype(BF16)

    pl.semaphore_wait(barrier, 6 + groups)

    ag_start(0, 0)
    cr_start(0)
    ag_start(0, 1)
    ag_forward(0, 0)
    dp_start(0, cr_total(0).astype(BF16))
    ag_forward(0, 1)
    request = lax.broadcasted_iota(jnp.int32, (nreq, nreq), 0)
    holder = (request == deal_ref[...]).astype(F32).astype(BF16)
    member = lax.broadcasted_iota(jnp.int32, (slots, nreq), 0) + slots * g
    listed = lax.broadcasted_iota(jnp.int32, (slots, nreq), 1)
    picker = lax.dot_general(
        (member == listed).astype(F32).astype(BF16), holder, NT, preferred_element_type=F32
    ).astype(BF16)
    ag_far(0, 0)
    ag_finish(0, 0)
    local["qkv"].wait()
    project(0)
    ag_far(0, 1)
    chooser = (member == deal_ref[...]).astype(F32).astype(BF16)
    ca_start(0, jnp.dot(chooser, dp_total(0), preferred_element_type=F32).astype(BF16))
    ag_finish(0, 1)
    project(1)
    local["pk"].wait()
    local["pv"].wait()
    local["out"].wait()
    attend(0, 0)
    attend(0, 1)
    out_project(0)
    attend(1, 0)
    for n in range(CHUNKS):
        rs_combine(0, 0, n)
    attend(1, 1)
    for n in range(CHUNKS):
        rs_relay(0, 0, n)
    out_project(1)
    ca_finish(0)
    decode_project()
    for n in range(CHUNKS):
        rs_combine(0, 1, n)
    middle(0)
    for n in range(CHUNKS):
        rs_relay(0, 1, n)
    local["dk"].wait()
    local["dv"].wait()
    decode_attend()
    cr_start(1)
    ag_forward(1, 0)
    middle(1)
    total = dag[0, :, columns(t)].astype(F32) + cr_total(1)
    ca_start(1, total.astype(BF16))
    ag_far(1, 0)
    ag_forward(1, 1)
    ca_finish(1)
    xg2[0, 8 * HALF :, :] = normed(dag[1].astype(F32), fgain_ref[...])
    local["gate"].wait()
    local["up"].wait()
    local["down"].wait()
    ag_finish(1, 0)
    gated(0)
    ag_far(1, 1)
    lower(0)
    cr_start(2)
    for n in range(CHUNKS):
        rs_combine(1, 0, n)
    ag_finish(1, 1)
    gated(1)
    for n in range(CHUNKS):
        rs_relay(1, 0, n)
    total = dag[1, :, columns(t)].astype(F32) + cr_total(2)
    dp_start(1, total.astype(BF16))
    lower(1)
    for n in range(CHUNKS):
        rs_combine(1, 1, n)
    ca_start(2, jnp.dot(picker, dp_total(1), preferred_element_type=F32).astype(BF16))
    for n in range(CHUNKS):
        rs_relay(1, 1, n)
    last(0)
    last(1)
    ca_finish(2)
    every = dag[2].astype(F32)
    first = jnp.sum(jnp.where(spot == 2 * t, every, 0.0), axis=0, keepdims=True)
    second = jnp.sum(jnp.where(spot == 2 * t + 1, every, 0.0), axis=0, keepdims=True)
    dout_ref[...] = jnp.concatenate([first, second], axis=0).astype(BF16)

    for copy in sends:
        copy.wait_send()


def rotary_tables(places):
    lane = jnp.arange(HD, dtype=jnp.int32)
    powers = (lane % (HD // 2)).astype(F32) * (2.0 / HD)
    angles = places.astype(F32)[:, None] * (THETA ** (-powers))[None, :]
    sign = jnp.where(lane < HD // 2, -1.0, 1.0).astype(F32)
    return jnp.cos(angles), jnp.sin(angles) * sign[None, :]


def on_device(
    groups,
    prefill_rows,
    decode_rows,
    deal_order,
    prefill_offset,
    cache_length,
    prefill_cache,
    decode_cache,
    qkv_weight,
    out_weight,
    attention_gain,
    forward_gain,
    gate_weight,
    up_weight,
    down_weight,
):
    width = prefill_rows.shape[1]
    fresh = 8 * prefill_rows.shape[0]
    slots = cache_length.shape[0]
    stored = prefill_cache.shape[2]
    dstored = decode_cache.shape[2]
    units = gate_weight.shape[1]
    places = jnp.concatenate(
        [prefill_offset[0] + jnp.arange(fresh, dtype=jnp.int32), cache_length]
    )
    cosine, sine = rotary_tables(places)
    cw = width // CHUNKS
    bw = width // 8
    vmem = pl.BlockSpec(memory_space=pltpu.VMEM)
    smem = pl.BlockSpec(memory_space=pltpu.SMEM)
    hbm = pl.BlockSpec(memory_space=pl.ANY)
    dma = pltpu.SemaphoreType.DMA
    shape = jax.ShapeDtypeStruct
    return pl.pallas_call(
        functools.partial(layer_kernel, groups),
        name="layer",
        out_shape=(
            shape(prefill_rows.shape, BF16),
            shape(decode_rows.shape, BF16),
            shape((2, fresh, HD), BF16),
            shape((2, slots, HD), BF16),
        ),
        in_specs=[vmem, vmem, vmem, smem, smem, vmem, vmem, vmem, vmem] + [hbm] * 7,
        out_specs=(vmem, vmem, vmem, vmem),
        scratch_shapes=[
            pltpu.VMEM((width, 4 * HD), BF16),
            pltpu.VMEM((2 * HD, width), BF16),
            pltpu.VMEM((width, units), BF16),
            pltpu.VMEM((width, units), BF16),
            pltpu.VMEM((units, width), BF16),
            pltpu.VMEM((stored + fresh, HD), BF16),
            pltpu.VMEM((stored + fresh, HD), BF16),
            pltpu.VMEM((slots, dstored, HD), BF16),
            pltpu.VMEM((slots, dstored, HD), BF16),
            pltpu.VMEM((2, 8 * HALF, width), BF16),
            pltpu.VMEM((2, 8 * HALF + slots, width), BF16),
            pltpu.VMEM((8 * HALF, 4 * HD), F32),
            pltpu.VMEM((2, 2, 8 * HALF, HD), BF16),
            pltpu.VMEM((2, 8 * HALF, 2 * HD), BF16),
            pltpu.VMEM((2, 2, CHUNKS, 2, 4, HALF, cw), BF16),
            pltpu.VMEM((2, 2, CHUNKS, 4, HALF, cw), BF16),
            pltpu.VMEM((2, 2, CHUNKS, 4, HALF, cw), BF16),
            pltpu.VMEM((2, 2, CHUNKS, HALF, cw), BF16),
            pltpu.VMEM((2, 2, CHUNKS, 2, HALF, cw), BF16),
            pltpu.VMEM(prefill_rows.shape, BF16),
            pltpu.VMEM((2, 8 * HALF + slots, units), BF16),
            pltpu.VMEM((3, slots, width), BF16),
            pltpu.VMEM((3, 8, slots, bw), BF16),
            pltpu.VMEM((2, groups, slots, bw), BF16),
            pltpu.VMEM((3, slots, width), BF16),
            pltpu.VMEM((16 * slots, dstored + HD), F32),
            pltpu.VMEM((16 * slots, dstored + HD), BF16),
            pltpu.VMEM((16 * slots, HD), BF16),
            pltpu.VMEM((HD, HD), BF16),
            pltpu.VMEM((HD, HD), BF16),
            pltpu.VMEM((16 * slots, HD), F32),
            dma((9,)),
            dma((2, 2, 14)),
            dma((2, 2, 14)),
            dma((2, 2, CHUNKS, 4)),
            dma((2, 2, CHUNKS, 4)),
            dma((3, 8)),
            dma((3, 8)),
            dma((2, groups)),
            dma((2, groups)),
            dma((3, 8)),
            dma((3, 8)),
        ],
        compiler_params=pltpu.CompilerParams(
            collective_id=0, has_side_effects=True, vmem_limit_bytes=66_000_000
        ),
    )(
        prefill_rows,
        decode_rows,
        deal_order[None, :],
        prefill_offset,
        cache_length,
        cosine,
        sine,
        attention_gain[None, :],
        forward_gain[None, :],
        prefill_cache,
        decode_cache,
        qkv_weight.reshape(width, 4 * HD),
        out_weight,
        gate_weight,
        up_weight,
        down_weight,
    )


def solution(mesh):
    placed = (
        P(("dp", "tensor"), None),
        P(("dp", "tensor"), None),
        P(),
        P("dp"),
        P("dp"),
        P(None, "dp", None, "tensor"),
        P(None, "dp", None, "tensor"),
        P(None, "tensor", None),
        P("tensor", None),
        P(),
        P(),
        P(None, "tensor"),
        P(None, "tensor"),
        P("tensor", None),
    )
    return jax.shard_map(
        functools.partial(on_device, mesh.shape["dp"]),
        mesh=mesh,
        in_specs=placed,
        out_specs=(
            P(("dp", "tensor"), None),
            P(("dp", "tensor"), None),
            P(None, "dp", "tensor"),
            P(None, "dp", "tensor"),
        ),
        check_vma=False,
    )
```

```python
import functools
import math

import jax
import jax.numpy as jnp
from jax import lax
from jax.experimental import pallas as pl
from jax.experimental.pallas import tpu as pltpu
from jax.sharding import PartitionSpec as P

HD = 128
EPSILON = 1e-06
THETA = 1000000.0
NEGATIVE = -1e30
MESH = pl.DeviceIdType.MESH
F32 = jnp.float32
BF16 = jnp.bfloat16
NT = (((1,), (1,)), ((), ()))
BATCHES = 4
SIZE = 16
JOINED = 1
CHUNKS = 2


def normed(values, gain):
    spread = jnp.mean(values * values, axis=-1, keepdims=True)
    return (values * lax.rsqrt(spread + EPSILON) * gain).astype(BF16)


def layer_kernel(
    groups,
    rows_ref,
    drows_ref,
    deal_ref,
    off_ref,
    len_ref,
    again_ref,
    fgain_ref,
    pcache,
    dcache,
    qkv_hbm,
    out_hbm,
    gate_hbm,
    up_hbm,
    down_hbm,
    pout_ref,
    dout_ref,
    pent_ref,
    dent_ref,
    w_qkv,
    w_out,
    w_gate,
    w_up,
    w_down,
    kall,
    vall,
    kdec,
    vdec,
    xg1,
    xg2,
    kplace,
    dtotal,
    qb,
    att,
    pb,
    rcv,
    cb,
    fb,
    nb,
    resid,
    hid,
    dpart,
    drs,
    dpb,
    dag,
    dsc,
    dpr,
    qpad,
    knew,
    vnew,
    dob,
    cos_ref,
    sin_ref,
    wsem,
    ags,
    agr,
    rss,
    rsr,
    crs,
    crr,
    dps,
    dpr_sem,
    cas,
    car,
):
    g = lax.axis_index("dp")
    t = lax.axis_index("tensor")
    x = t // 2
    c = t % 2
    width = rows_ref.shape[1]
    cw = width // CHUNKS
    bw = width // 8
    stored = pcache.shape[2]
    fresh = pent_ref.shape[1]
    slots = dent_ref.shape[1]
    dstored = dcache.shape[2]
    units = w_gate.shape[1]
    nreq = groups * slots
    scale2 = (1.0 / math.sqrt(HD)) * math.log2(math.e)

    partner = (g, t + 1 - 2 * c)
    right = (g, ((x + 1) % 4) * 2 + c)
    left = (g, ((x + 3) % 4) * 2 + c)
    sends = []

    def remote(src, dst, ss, rs, dev):
        copy = pltpu.make_async_remote_copy(
            src_ref=src, dst_ref=dst, send_sem=ss, recv_sem=rs, device_id=dev, device_id_type=MESH
        )
        copy.start()
        sends.append(copy)

    def arrived(dst, ss, rs):
        pltpu.make_async_remote_copy(
            src_ref=dst, dst_ref=dst, send_sem=ss, recv_sem=rs, device_id=partner, device_id_type=MESH
        ).wait_recv()

    local = {}

    def fetch(name, index, src, dst):
        copy = pltpu.make_async_copy(src, dst, wsem.at[index])
        copy.start()
        local[name] = copy

    fetch("qkv", 0, qkv_hbm, w_qkv)
    fetch("pk", 1, pcache.at[0, 0], kall.at[pl.ds(0, stored)])
    fetch("pv", 2, pcache.at[1, 0], vall.at[pl.ds(0, stored)])
    fetch("out", 3, out_hbm, w_out)
    fetch("dk", 4, dcache.at[0], kdec)
    fetch("dv", 5, dcache.at[1], vdec)
    fetch("gate", 6, gate_hbm, w_gate)
    fetch("up", 7, up_hbm, w_up)
    fetch("down", 8, down_hbm, w_down)

    barrier = pltpu.get_barrier_semaphore()
    for k in range(1, 8):
        pl.semaphore_signal(barrier, inc=1, device_id=(g, (t + k) % 8), device_id_type=MESH)
    for k in range(1, groups):
        pl.semaphore_signal(barrier, inc=1, device_id=((g + k) % groups, t), device_id_type=MESH)

    def buffer_of(stage, h):
        return (xg1 if stage == 0 else xg2).at[h]

    def ag_block(stage, h, b, p):
        rows = pl.ds(SIZE * b, SIZE)
        if p is None:
            return buffer_of(stage, h).at[rows]
        return buffer_of(stage, h).at[rows, pl.ds(width // 2 * p, width // 2)]

    def ag_send(stage, h, src_b, dst_b, p, number, dev):
        remote(
            ag_block(stage, h, src_b, p),
            ag_block(stage, h, dst_b, p),
            ags.at[stage, h, number],
            agr.at[stage, h, number],
            dev,
        )

    def ag_wait(stage, h, b, p, number):
        arrived(ag_block(stage, h, b, p), ags.at[stage, h, number], agr.at[stage, h, number])

    def ag_start(stage, h):
        ag_send(stage, h, 0, 4, 0, 1, right)
        ag_send(stage, h, 0, 2, 1, 4, left)
        ag_send(stage, h, 0, 4, 1, 2, right)
        ag_send(stage, h, 0, 2, 0, 3, left)
        ag_send(stage, h, 0, 1, None, 0, partner)

    def ag_onward(stage, h):
        ag_wait(stage, h, 4, 0, 1)
        ag_send(stage, h, 4, 6, 0, 5, right)
        ag_wait(stage, h, 2, 1, 4)
        ag_send(stage, h, 2, 6, 1, 6, left)

    def ag_share(stage, h):
        ag_wait(stage, h, 4, 1, 2)
        ag_send(stage, h, 4, 5, None, 7, partner)
        ag_wait(stage, h, 2, 0, 3)
        ag_send(stage, h, 2, 3, None, 8, partner)

    def ag_far(stage, h):
        ag_wait(stage, h, 6, 0, 5)
        ag_wait(stage, h, 6, 1, 6)
        ag_send(stage, h, 6, 7, None, 9, partner)

    def ag_finish(stage, h):
        for b, number in ((1, 0), (5, 7), (3, 8), (7, 9)):
            ag_wait(stage, h, b, None, number)

    def rs_split(stage, h, n, part):
        for b in range(8):
            pb[stage, h, n, b % 2, b // 2] = part[SIZE * b : SIZE * (b + 1)].astype(BF16)
        remote(
            pb.at[stage, h, n, 1],
            rcv.at[stage, h, n],
            rss.at[stage, h, n, 0],
            rsr.at[stage, h, n, 0],
            partner,
        )

    def on_chip(stage, h, n, d):
        return pb[stage, h, n, 0, d].astype(F32) + rcv[stage, h, n, d].astype(F32)

    def to_side(stage, h, n, d):
        side, dev = (0, right) if d == 1 else (1, left)
        remote(
            cb.at[stage, h, n, d],
            nb.at[stage, h, n, side],
            rss.at[stage, h, n, 2 + side],
            rsr.at[stage, h, n, 2 + side],
            dev,
        )

    def rs_combine(stage, h):
        for n in range(CHUNKS):
            rs_combine_chunk(stage, h, n)

    def rs_relay(stage, h):
        for n in range(CHUNKS):
            rs_relay_chunk(stage, h, n)

    def rs_combine_chunk(stage, h, n):
        arrived(rcv.at[stage, h, n], rss.at[stage, h, n, 0], rsr.at[stage, h, n, 0])
        cb[stage, h, n, 3] = on_chip(stage, h, n, 3).astype(BF16)
        remote(
            cb.at[stage, h, n, 3],
            fb.at[stage, h, n],
            rss.at[stage, h, n, 1],
            rsr.at[stage, h, n, 1],
            right if n % 2 == 0 else left,
        )
        d = 2 if n % 2 == 0 else 1
        cb[stage, h, n, d] = on_chip(stage, h, n, d).astype(BF16)
        to_side(stage, h, n, d)

    def rs_relay_chunk(stage, h, n):
        arrived(fb.at[stage, h, n], rss.at[stage, h, n, 1], rsr.at[stage, h, n, 1])
        d = 1 if n % 2 == 0 else 2
        cb[stage, h, n, d] = (on_chip(stage, h, n, d) + fb[stage, h, n].astype(F32)).astype(BF16)
        to_side(stage, h, n, d)

    def rs_total(stage, h, n):
        for side in range(2):
            arrived(
                nb.at[stage, h, n, side],
                rss.at[stage, h, n, 2 + side],
                rsr.at[stage, h, n, 2 + side],
            )
        return (
            on_chip(stage, h, n, 0) + nb[stage, h, n, 0].astype(F32) + nb[stage, h, n, 1].astype(F32)
        )

    def columns(p):
        return pl.ds(pl.multiple_of(p * bw, bw), bw)

    def cr_start(i):
        for k in range(1, 8):
            p = (t + k) % 8
            remote(
                dpart.at[i, :, columns(p)], drs.at[i, k], crs.at[i, k], crr.at[i, k], (g, p)
            )

    def cr_total(i):
        total = dpart[i, :, columns(t)].astype(F32)
        for k in range(1, 8):
            arrived(drs.at[i, k], crs.at[i, k], crr.at[i, k])
            total = total + drs[i, k].astype(F32)
        return total

    def dp_start(i, block):
        dpb[i, g] = block
        for k in range(1, groups):
            remote(
                dpb.at[i, g], dpb.at[i, g], dps.at[i, k], dpr_sem.at[i, k], ((g + k) % groups, t)
            )

    def dp_total(i):
        for k in range(1, groups):
            source = (g + groups - k) % groups
            arrived(dpb.at[i, source], dps.at[i, k], dpr_sem.at[i, k])
        return dpb[i].reshape(nreq, bw)

    def ca_start(i, block):
        dag[i, :, columns(t)] = block
        for k in range(1, 8):
            mine = dag.at[i, :, columns(t)]
            remote(mine, mine, cas.at[i, k], car.at[i, k], (g, (t + k) % 8))

    def ca_finish(i):
        for k in range(1, 8):
            arrived(dag.at[i, :, columns((t + 8 - k) % 8)], cas.at[i, k], car.at[i, k])

    def rotated(part, cosine, sine):
        return part * cosine + pltpu.roll(part, HD // 2, 1) * sine

    def owner_of(b):
        d = b // 2
        return 2 * ((x + d + (d // 2) * (5 - 2 * d)) % 4) + (c + b % 2) % 2

    part_rows = 8 * SIZE

    def place_of(index):
        b = (index // SIZE) % 8
        d = b >> 1
        owner = 2 * ((x + (d ^ (d >> 1))) & 3) + ((c + (b & 1)) & 1)
        return owner * (BATCHES * SIZE) + SIZE * (index // part_rows) + index % SIZE

    def project(h):
        part = jnp.dot(xg1[h], w_qkv[...], preferred_element_type=F32)
        here = slice(part_rows * h, part_rows * (h + 1))
        there = slice(stored + part_rows * h, stored + part_rows * (h + 1))
        cosine = cos_ref[here, :]
        sine = sin_ref[here, :]
        for head in range(2):
            qb[h, head] = rotated(part[:, HD * head : HD * (head + 1)], cosine, sine).astype(BF16)
        kall[there, :] = rotated(part[:, 2 * HD : 3 * HD], cosine, sine).astype(BF16)
        vall[there, :] = part[:, 3 * HD : 4 * HD].astype(BF16)

    def entries(h):
        for b in range(8):
            first = pl.multiple_of(owner_of(b) * (BATCHES * SIZE) + SIZE * h, SIZE)
            here = pl.ds(stored + part_rows * h + SIZE * b, SIZE)
            pent_ref[0, pl.ds(first, SIZE), :] = kall[here, :]
            pent_ref[1, pl.ds(first, SIZE), :] = vall[here, :]

    def attend(h):
        rows = part_rows
        query = qb[h].reshape(2 * rows, HD)
        scores = lax.dot_general(query, kall[...], NT, preferred_element_type=F32)
        r = lax.broadcasted_iota(jnp.int32, (2 * rows, 1), 0)
        q_place = place_of(rows * h + r % rows)
        k_place = kplace[...]
        scores = jnp.where(k_place <= q_place, scores, NEGATIVE)
        top = jnp.max(scores, axis=-1, keepdims=True)
        weights = jnp.exp2((scores - top) * scale2)
        total = jnp.sum(weights, axis=-1, keepdims=True)
        result = jnp.dot(weights.astype(BF16), vall[...], preferred_element_type=F32)
        result = (result / total).astype(BF16)
        att[h, :, 0:HD] = result[:rows]
        att[h, :, HD : 2 * HD] = result[rows:]

    def out_project(h, n):
        part = jnp.dot(att[h], w_out[:, cw * n : cw * (n + 1)], preferred_element_type=F32)
        rs_split(0, h, n, part)

    def middle(h):
        mine = pl.ds(SIZE * h, SIZE)
        pieces = []
        for n in range(CHUNKS):
            cols = slice(cw * n, cw * (n + 1))
            value = (rows_ref[mine, cols].astype(F32) + rs_total(0, h, n)).astype(BF16)
            resid[mine, cols] = value
            pieces.append(value.astype(F32))
        values = jnp.concatenate(pieces, axis=1)
        xg2[h, 0:SIZE, :] = normed(values, fgain_ref[...])
        ag_start(1, h)

    steps = units // 256

    def gated(h, begin=0, end=steps):
        count = 8 * SIZE + (slots if h == JOINED else 0)
        step = 256

        def one(j, carry):
            cols = pl.ds(pl.multiple_of(j * step, step), step)
            inner = xg2[h, 0:count, :]
            gate_part = jnp.dot(inner, w_gate[:, cols], preferred_element_type=F32)
            up_part = jnp.dot(inner, w_up[:, cols], preferred_element_type=F32)
            hid[0:count, cols] = (
                gate_part / (1.0 + jnp.exp(-gate_part)) * up_part
            ).astype(BF16)
            return carry

        lax.fori_loop(begin, end, one, 0)

    def lower(h, n):
        count = 8 * SIZE + (slots if h == JOINED else 0)
        cols = slice(cw * n, cw * (n + 1))
        part = jnp.dot(hid[0:count, :], w_down[:, cols], preferred_element_type=F32)
        rs_split(1, h, n, part)
        if h == JOINED:
            dpart[2, :, cols] = part[8 * SIZE :].astype(BF16)

    def last(h):
        mine = pl.ds(SIZE * h, SIZE)
        for n in range(CHUNKS):
            cols = slice(cw * n, cw * (n + 1))
            pout_ref[mine, cols] = (resid[mine, cols].astype(F32) + rs_total(1, h, n)).astype(BF16)

    wide = 16 * slots

    def marker(head, flip):
        shape = (slots, wide) if flip else (wide, slots)
        row = lax.broadcasted_iota(jnp.int32, shape, 1 if flip else 0)
        slot = lax.broadcasted_iota(jnp.int32, shape, 0 if flip else 1)
        return (row == 16 * slot + head).astype(F32).astype(BF16)

    def decode_project():
        inner = normed(dag[0].astype(F32), again_ref[...])
        part = jnp.dot(inner, w_qkv[...], preferred_element_type=F32)
        cosine = cos_ref[fresh : fresh + slots, :]
        sine = sin_ref[fresh : fresh + slots, :]
        spread = jnp.zeros((wide, HD), F32)
        for head in range(2):
            query = rotated(part[:, HD * head : HD * (head + 1)], cosine, sine).astype(BF16)
            spread = spread + jnp.dot(marker(head, False), query, preferred_element_type=F32)
        qpad[...] = spread.astype(BF16)
        key = rotated(part[:, 2 * HD : 3 * HD], cosine, sine).astype(BF16)
        value = part[:, 3 * HD : 4 * HD].astype(BF16)
        dent_ref[0] = key
        dent_ref[1] = value
        knew[...] = jnp.zeros_like(knew)
        vnew[...] = jnp.zeros_like(vnew)
        knew[0:slots, :] = key
        vnew[0:slots, :] = value

    def decode_attend(begin, end):
        def score(n, carry):
            here = pl.ds(pl.multiple_of(16 * n, 16), 16)
            part = lax.dot_general(qpad[here, :], kdec[n], NT, preferred_element_type=F32)
            col = lax.broadcasted_iota(jnp.int32, (16, dstored), 1)
            dsc[here, 0:dstored] = jnp.where(col < len_ref[n], part, NEGATIVE)
            return carry

        lax.fori_loop(begin, end, score, 0, unroll=4)

    def decode_weigh():
        own = lax.dot_general(qpad[...], knew[...], NT, preferred_element_type=F32)
        row = lax.broadcasted_iota(jnp.int32, (wide, HD), 0)
        col = lax.broadcasted_iota(jnp.int32, (wide, HD), 1)
        dsc[:, dstored:] = jnp.where(col == (row >> 4), own, NEGATIVE)
        scores = dsc[...]
        top = jnp.max(scores, axis=-1, keepdims=True)
        weights = jnp.exp2((scores - top) * scale2)
        dtotal[...] = jnp.sum(weights, axis=-1, keepdims=True)
        dpr[...] = weights.astype(BF16)

    def decode_mix():
        def mix(n, carry):
            here = pl.ds(pl.multiple_of(16 * n, 16), 16)
            dob[here, :] = jnp.dot(dpr[here, 0:dstored], vdec[n], preferred_element_type=F32)
            return carry

        lax.fori_loop(0, slots, mix, 0, unroll=4)
        result = dob[...] + jnp.dot(dpr[:, dstored:], vnew[...], preferred_element_type=F32)
        result = (result / dtotal[...]).astype(BF16)
        picked = [
            jnp.dot(marker(head, True), result, preferred_element_type=F32).astype(BF16)
            for head in range(2)
        ]
        attended = jnp.concatenate(picked, axis=1)
        dpart[1] = jnp.dot(attended, w_out[...], preferred_element_type=F32).astype(BF16)

    for h in range(BATCHES):
        mine = pl.ds(SIZE * h, SIZE)
        xg1[h, 0:SIZE, :] = normed(rows_ref[mine, :].astype(F32), again_ref[...])
    pair = drows_ref[...].astype(F32)
    spot = lax.broadcasted_iota(jnp.int32, (slots, width), 0)
    dpart[0] = (
        jnp.where(spot == 2 * t, pair[0:1], 0.0) + jnp.where(spot == 2 * t + 1, pair[1:2], 0.0)
    ).astype(BF16)

    lane = lax.broadcasted_iota(jnp.int32, (1, HD), 1)
    powers = (lane % (HD // 2)).astype(F32) * (2.0 / HD)
    inverse = jnp.exp(powers * (-math.log(THETA)))
    sign = jnp.where(lane < HD // 2, -1.0, 1.0).astype(F32)

    def table(first, count, places):
        angles = places.astype(F32) * inverse
        cos_ref[pl.ds(first, count), :] = jnp.cos(angles)
        sin_ref[pl.ds(first, count), :] = jnp.sin(angles) * sign

    def some(i, carry):
        row = lax.broadcasted_iota(jnp.int32, (64, HD), 0)
        table(pl.multiple_of(64 * i, 64), 64, off_ref[0] + place_of(64 * i + row))
        return carry

    lax.fori_loop(0, fresh // 64, some, 0)
    col = lax.broadcasted_iota(jnp.int32, (1, stored + fresh), 1)
    kplace[...] = jnp.where(
        col < stored,
        jnp.where(col < off_ref[0], -1, fresh),
        place_of(jnp.maximum(col - stored, 0)),
    )
    slot = lax.broadcasted_iota(jnp.int32, (slots, HD), 0)
    length = jnp.zeros((slots, HD), jnp.int32)
    for n in range(slots):
        length = jnp.where(slot == n, len_ref[n], length)
    table(fresh, slots, length)

    request = lax.broadcasted_iota(jnp.int32, (nreq, nreq), 0)
    holder = (request == deal_ref[...]).astype(F32).astype(BF16)
    member = lax.broadcasted_iota(jnp.int32, (slots, nreq), 0) + slots * g
    listed = lax.broadcasted_iota(jnp.int32, (slots, nreq), 1)
    picker = lax.dot_general(
        (member == listed).astype(F32).astype(BF16), holder, NT, preferred_element_type=F32
    ).astype(BF16)
    chooser = (member == deal_ref[...]).astype(F32).astype(BF16)

    def dealt():
        ca_start(0, jnp.dot(chooser, dp_total(0), preferred_element_type=F32).astype(BF16))

    def decode_middle():
        total = dag[0, :, columns(t)].astype(F32) + cr_total(1)
        ca_start(1, total.astype(BF16))

    def decode_inner():
        ca_finish(1)
        xg2[JOINED, part_rows:, :] = normed(dag[1].astype(F32), fgain_ref[...])

    def decode_last():
        total = dag[1, :, columns(t)].astype(F32) + cr_total(2)
        dp_start(1, total.astype(BF16))

    def undealt():
        ca_start(2, jnp.dot(picker, dp_total(1), preferred_element_type=F32).astype(BF16))

    def decode_out():
        ca_finish(2)
        every = dag[2].astype(F32)
        first = jnp.sum(jnp.where(spot == 2 * t, every, 0.0), axis=0, keepdims=True)
        second = jnp.sum(jnp.where(spot == 2 * t + 1, every, 0.0), axis=0, keepdims=True)
        dout_ref[...] = jnp.concatenate([first, second], axis=0).astype(BF16)

    pl.semaphore_wait(barrier, 6 + groups)

    ag_start(0, 0)
    ag_start(0, 1)
    cr_start(0)
    ag_start(0, 2)
    ag_start(0, 3)
    ag_onward(0, 0)
    ag_share(0, 0)
    ag_onward(0, 1)
    ag_share(0, 1)
    ag_onward(0, 2)
    dp_start(0, cr_total(0).astype(BF16))
    ag_share(0, 2)
    ag_onward(0, 3)
    ag_share(0, 3)
    ag_far(0, 0)
    ag_far(0, 1)
    local["qkv"].wait()
    ag_finish(0, 0)
    project(0)
    ag_far(0, 2)
    dealt()
    ag_finish(0, 1)
    project(1)
    ag_far(0, 3)
    entries(1)
    entries(0)
    ag_finish(0, 2)
    project(2)
    entries(2)
    ag_finish(0, 3)
    project(3)
    local["pk"].wait()
    local["pv"].wait()
    local["out"].wait()
    attend(0)
    out_project(0, 0)
    out_project(0, 1)
    attend(1)
    out_project(1, 0)
    entries(3)
    out_project(1, 1)
    rs_combine(0, 0)
    ca_finish(0)
    decode_project()
    local["dk"].wait()
    decode_attend(0, slots // 2)
    rs_combine(0, 1)
    attend(2)
    out_project(2, 0)
    out_project(2, 1)
    attend(3)
    rs_relay(0, 0)
    out_project(3, 0)
    out_project(3, 1)
    rs_combine(0, 2)
    decode_attend(slots // 2, slots)
    decode_weigh()
    rs_relay(0, 1)
    rs_combine(0, 3)
    local["dv"].wait()
    decode_mix()
    middle(0)
    cr_start(1)
    rs_relay(0, 2)
    middle(1)
    rs_relay(0, 3)
    ag_onward(1, 0)
    ag_share(1, 0)
    middle(2)
    decode_middle()
    ag_onward(1, 1)
    ag_share(1, 1)
    middle(3)
    ag_far(1, 0)
    ag_onward(1, 2)
    local["gate"].wait()
    local["up"].wait()
    local["down"].wait()
    ag_finish(1, 0)
    gated(0, 0, steps // 2)
    ag_share(1, 2)
    gated(0, steps // 2, steps)
    ag_far(1, 1)
    lower(0, 0)
    decode_inner()
    lower(0, 1)
    ag_onward(1, 3)
    ag_finish(1, 1)
    gated(1, 0, steps // 2)
    gated(1, steps // 2, steps)
    ag_far(1, 2)
    rs_combine(1, 0)
    lower(1, 0)
    lower(1, 1)
    cr_start(2)
    ag_share(1, 3)
    ag_finish(1, 2)
    gated(2, 0, steps // 2)
    ag_far(1, 3)
    gated(2, steps // 2, steps)
    rs_combine(1, 1)
    lower(2, 0)
    lower(2, 1)
    ag_finish(1, 3)
    gated(3, 0, steps // 2)
    rs_relay(1, 0)
    gated(3, steps // 2, steps)
    rs_combine(1, 2)
    lower(3, 0)
    decode_last()
    lower(3, 1)
    rs_relay(1, 1)
    last(0)
    rs_combine(1, 3)
    rs_relay(1, 2)
    last(1)
    undealt()
    rs_relay(1, 3)
    last(2)
    decode_out()
    last(3)

    for copy in sends:
        copy.wait_send()


def hand_out(*refs):
    count = len(refs) // 3 + 1
    sources, targets, sems = refs[:count], refs[count : 2 * count], refs[2 * count]
    copies = [
        pltpu.make_async_copy(source, target, sems.at[i])
        for i, (source, target) in enumerate(zip(sources, targets))
    ]
    for copy in copies:
        copy.start()
    for copy in copies:
        copy.wait()


def on_device(
    groups,
    prefill_rows,
    decode_rows,
    deal_order,
    prefill_offset,
    cache_length,
    prefill_cache,
    decode_cache,
    qkv_weight,
    out_weight,
    attention_gain,
    forward_gain,
    gate_weight,
    up_weight,
    down_weight,
):
    width = prefill_rows.shape[1]
    fresh = 8 * prefill_rows.shape[0]
    slots = cache_length.shape[0]
    stored = prefill_cache.shape[2]
    dstored = decode_cache.shape[2]
    units = gate_weight.shape[1]
    cw = width // CHUNKS
    bw = width // 8
    vmem = pl.BlockSpec(memory_space=pltpu.VMEM)
    smem = pl.BlockSpec(memory_space=pltpu.SMEM)
    hbm = pl.BlockSpec(memory_space=pl.ANY)
    dma = pltpu.SemaphoreType.DMA
    shape = jax.ShapeDtypeStruct
    results = pl.pallas_call(
        functools.partial(layer_kernel, groups),
        name="layer",
        out_shape=(
            shape(prefill_rows.shape, BF16),
            shape(decode_rows.shape, BF16),
            shape((2, fresh, HD), BF16),
            shape((2, slots, HD), BF16),
        ),
        in_specs=[vmem, vmem, vmem, smem, smem, vmem, vmem] + [hbm] * 7,
        out_specs=(vmem, vmem, vmem, vmem),
        scratch_shapes=[
            pltpu.VMEM((width, 4 * HD), BF16),
            pltpu.VMEM((2 * HD, width), BF16),
            pltpu.VMEM((width, units), BF16),
            pltpu.VMEM((width, units), BF16),
            pltpu.VMEM((units, width), BF16),
            pltpu.VMEM((stored + fresh, HD), BF16),
            pltpu.VMEM((stored + fresh, HD), BF16),
            pltpu.VMEM((slots, dstored, HD), BF16),
            pltpu.VMEM((slots, dstored, HD), BF16),
            pltpu.VMEM((BATCHES, 8 * SIZE, width), BF16),
            pltpu.VMEM((BATCHES, 8 * SIZE + slots, width), BF16),
            pltpu.VMEM((1, stored + fresh), jnp.int32),
            pltpu.VMEM((16 * slots, 1), F32),
            pltpu.VMEM((BATCHES, 2, 8 * SIZE, HD), BF16),
            pltpu.VMEM((BATCHES, 8 * SIZE, 2 * HD), BF16),
            pltpu.VMEM((2, BATCHES, CHUNKS, 2, 4, SIZE, cw), BF16),
            pltpu.VMEM((2, BATCHES, CHUNKS, 4, SIZE, cw), BF16),
            pltpu.VMEM((2, BATCHES, CHUNKS, 4, SIZE, cw), BF16),
            pltpu.VMEM((2, BATCHES, CHUNKS, SIZE, cw), BF16),
            pltpu.VMEM((2, BATCHES, CHUNKS, 2, SIZE, cw), BF16),
            pltpu.VMEM(prefill_rows.shape, BF16),
            pltpu.VMEM((8 * SIZE + slots, units), BF16),
            pltpu.VMEM((3, slots, width), BF16),
            pltpu.VMEM((3, 8, slots, bw), BF16),
            pltpu.VMEM((2, groups, slots, bw), BF16),
            pltpu.VMEM((3, slots, width), BF16),
            pltpu.VMEM((16 * slots, dstored + HD), F32),
            pltpu.VMEM((16 * slots, dstored + HD), BF16),
            pltpu.VMEM((16 * slots, HD), BF16),
            pltpu.VMEM((HD, HD), BF16),
            pltpu.VMEM((HD, HD), BF16),
            pltpu.VMEM((16 * slots, HD), F32),
            pltpu.VMEM((fresh + slots, HD), F32),
            pltpu.VMEM((fresh + slots, HD), F32),
            dma((9,)),
            dma((2, BATCHES, 10)),
            dma((2, BATCHES, 10)),
            dma((2, BATCHES, CHUNKS, 4)),
            dma((2, BATCHES, CHUNKS, 4)),
            dma((3, 8)),
            dma((3, 8)),
            dma((2, groups)),
            dma((2, groups)),
            dma((3, 8)),
            dma((3, 8)),
        ],
        compiler_params=pltpu.CompilerParams(
            collective_id=0, has_side_effects=True, vmem_limit_bytes=66_000_000
        ),
    )(
        prefill_rows,
        decode_rows,
        deal_order[None, :],
        prefill_offset,
        cache_length,
        attention_gain[None, :],
        forward_gain[None, :],
        prefill_cache,
        decode_cache,
        qkv_weight.reshape(width, 4 * HD),
        out_weight,
        gate_weight,
        up_weight,
        down_weight,
    )
    return pl.pallas_call(
        hand_out,
        name="hand_out",
        out_shape=tuple(shape(result.shape, BF16) for result in results),
        in_specs=[vmem] * 4,
        out_specs=(hbm,) * 4,
        scratch_shapes=[dma((4,))],
    )(*results)


def solution(mesh):
    placed = (
        P(("dp", "tensor"), None),
        P(("dp", "tensor"), None),
        P(),
        P("dp"),
        P("dp"),
        P(None, "dp", None, "tensor"),
        P(None, "dp", None, "tensor"),
        P(None, "tensor", None),
        P("tensor", None),
        P(),
        P(),
        P(None, "tensor"),
        P(None, "tensor"),
        P("tensor", None),
    )
    return jax.shard_map(
        functools.partial(on_device, mesh.shape["dp"]),
        mesh=mesh,
        in_specs=placed,
        out_specs=(
            P(("dp", "tensor"), None),
            P(("dp", "tensor"), None),
            P(None, "dp", "tensor"),
            P(None, "dp", "tensor"),
        ),
        check_vma=False,
    )
```

```python
import functools
import math

import jax
import jax.numpy as jnp
from jax import lax
from jax.experimental import pallas as pl
from jax.experimental.pallas import tpu as pltpu
from jax.sharding import PartitionSpec as P

HD = 128
EPSILON = 1e-06
THETA = 1000000.0
NEGATIVE = -1e30
MESH = pl.DeviceIdType.MESH
F32 = jnp.float32
BF16 = jnp.bfloat16
NT = (((1,), (1,)), ((), ()))
BATCHES = 4
SIZE = 16
JOINED = 0
CHUNKS = 2


def normed(values, gain):
    spread = jnp.mean(values * values, axis=-1, keepdims=True)
    return (values * lax.rsqrt(spread + EPSILON) * gain).astype(BF16)


def layer_kernel(
    groups,
    rows_ref,
    drows_ref,
    deal_ref,
    off_ref,
    len_ref,
    again_ref,
    fgain_ref,
    pcache,
    dcache,
    qkv_hbm,
    out_hbm,
    gate_hbm,
    up_hbm,
    down_hbm,
    pout_ref,
    dout_ref,
    pent_ref,
    dent_ref,
    w_qkv,
    w_out,
    w_gate,
    w_up,
    w_down,
    kall,
    vall,
    kdec,
    vdec,
    xg1,
    xg2,
    kplace,
    picker,
    chooser,
    dtotal,
    qb,
    att,
    pb,
    rcv,
    cb,
    fb,
    nb,
    resid,
    hid,
    dpart,
    drs,
    dpb,
    dag,
    dsc,
    dpr,
    qpad,
    knew,
    vnew,
    dob,
    cos_ref,
    sin_ref,
    wsem,
    ags,
    agr,
    rss,
    rsr,
    crs,
    crr,
    dps,
    dpr_sem,
    cas,
    car,
    passed,
):
    g = lax.axis_index("dp")
    t = lax.axis_index("tensor")
    x = t // 2
    c = t % 2
    width = rows_ref.shape[1]
    cw = width // CHUNKS
    bw = width // 8
    stored = pcache.shape[2]
    fresh = pent_ref.shape[1]
    slots = dent_ref.shape[1]
    dstored = dcache.shape[2]
    units = w_gate.shape[1]
    nreq = groups * slots
    scale2 = (1.0 / math.sqrt(HD)) * math.log2(math.e)

    partner = (g, t + 1 - 2 * c)
    right = (g, ((x + 1) % 4) * 2 + c)
    left = (g, ((x + 3) % 4) * 2 + c)
    sends = []

    def remote(src, dst, ss, rs, dev):
        copy = pltpu.make_async_remote_copy(
            src_ref=src, dst_ref=dst, send_sem=ss, recv_sem=rs, device_id=dev, device_id_type=MESH
        )
        copy.start()
        sends.append(copy)

    def arrived(dst, ss, rs):
        pltpu.make_async_remote_copy(
            src_ref=dst, dst_ref=dst, send_sem=ss, recv_sem=rs, device_id=partner, device_id_type=MESH
        ).wait_recv()

    local = {}

    def fetch(name, index, src, dst):
        copy = pltpu.make_async_copy(src, dst, wsem.at[index])
        copy.start()
        local[name] = copy

    fetch("qkv", 0, qkv_hbm, w_qkv)
    fetch("pk", 1, pcache.at[0, 0], kall.at[pl.ds(0, stored)])
    fetch("pv", 2, pcache.at[1, 0], vall.at[pl.ds(0, stored)])
    fetch("out", 3, out_hbm, w_out)
    fetch("dk", 4, dcache.at[0], kdec)
    fetch("dv", 5, dcache.at[1], vdec)
    fetch("gate", 6, gate_hbm, w_gate)
    fetch("up", 7, up_hbm, w_up)
    fetch("down", 8, down_hbm, w_down)

    deep = min(4, groups)
    high = groups // deep
    below = [(g // deep) * deep + (g + k) % deep for k in range(1, deep)]
    across = [(g + deep * k) % groups for k in range(1, high)]
    barrier = pltpu.get_barrier_semaphore()
    for k in range(1, 8):
        pl.semaphore_signal(barrier, inc=1, device_id=(g, (t + k) % 8), device_id_type=MESH)
    for other in below + across:
        pl.semaphore_signal(barrier, inc=1, device_id=(other, t), device_id_type=MESH)

    def buffer_of(stage, h):
        return (xg1 if stage == 0 else xg2).at[h]

    def ag_block(stage, h, b, p):
        rows = pl.ds(SIZE * b, SIZE)
        if p is None:
            return buffer_of(stage, h).at[rows]
        return buffer_of(stage, h).at[rows, pl.ds(width // 2 * p, width // 2)]

    def ag_send(stage, h, src_b, dst_b, p, number, dev):
        remote(
            ag_block(stage, h, src_b, p),
            ag_block(stage, h, dst_b, p),
            ags.at[stage, h, number],
            agr.at[stage, h, number],
            dev,
        )

    def ag_wait(stage, h, b, p, number):
        arrived(ag_block(stage, h, b, p), ags.at[stage, h, number], agr.at[stage, h, number])

    def ag_start(stage, h):
        ag_send(stage, h, 0, 4, 0, 1, right)
        ag_send(stage, h, 0, 2, 1, 4, left)
        ag_send(stage, h, 0, 4, 1, 2, right)
        ag_send(stage, h, 0, 2, 0, 3, left)
        ag_send(stage, h, 0, 1, None, 0, partner)

    def ag_onward(stage, h):
        ag_wait(stage, h, 4, 0, 1)
        ag_send(stage, h, 4, 6, 0, 5, right)
        ag_wait(stage, h, 2, 1, 4)
        ag_send(stage, h, 2, 6, 1, 6, left)

    def ag_share(stage, h):
        ag_wait(stage, h, 4, 1, 2)
        ag_send(stage, h, 4, 5, None, 7, partner)
        ag_wait(stage, h, 2, 0, 3)
        ag_send(stage, h, 2, 3, None, 8, partner)

    def ag_far(stage, h):
        ag_wait(stage, h, 6, 0, 5)
        ag_wait(stage, h, 6, 1, 6)
        ag_send(stage, h, 6, 7, None, 9, partner)

    def ag_finish(stage, h):
        for b, number in ((1, 0), (5, 7), (3, 8), (7, 9)):
            ag_wait(stage, h, b, None, number)

    def rs_split(stage, h, n, part):
        for b in range(8):
            pb[stage, h, n, b % 2, b // 2] = part[SIZE * b : SIZE * (b + 1)].astype(BF16)
        remote(
            pb.at[stage, h, n, 1],
            rcv.at[stage, h, n],
            rss.at[stage, h, n, 0],
            rsr.at[stage, h, n, 0],
            partner,
        )

    def on_chip(stage, h, n, d):
        return pb[stage, h, n, 0, d].astype(F32) + rcv[stage, h, n, d].astype(F32)

    def to_side(stage, h, n, d):
        side, dev = (0, right) if d == 1 else (1, left)
        remote(
            cb.at[stage, h, n, d],
            nb.at[stage, h, n, side],
            rss.at[stage, h, n, 2 + side],
            rsr.at[stage, h, n, 2 + side],
            dev,
        )

    def rs_combine(stage, h):
        for n in range(CHUNKS):
            arrived(rcv.at[stage, h, n], rss.at[stage, h, n, 0], rsr.at[stage, h, n, 0])
            cb[stage, h, n, 3] = on_chip(stage, h, n, 3).astype(BF16)
            remote(
                cb.at[stage, h, n, 3],
                fb.at[stage, h, n],
                rss.at[stage, h, n, 1],
                rsr.at[stage, h, n, 1],
                right if n % 2 == 0 else left,
            )
        for n in range(CHUNKS):
            d = 2 if n % 2 == 0 else 1
            cb[stage, h, n, d] = on_chip(stage, h, n, d).astype(BF16)
            to_side(stage, h, n, d)

    def rs_relay(stage, h):
        for n in range(CHUNKS):
            rs_relay_chunk(stage, h, n)

    def rs_relay_chunk(stage, h, n):
        arrived(fb.at[stage, h, n], rss.at[stage, h, n, 1], rsr.at[stage, h, n, 1])
        d = 1 if n % 2 == 0 else 2
        cb[stage, h, n, d] = (on_chip(stage, h, n, d) + fb[stage, h, n].astype(F32)).astype(BF16)
        to_side(stage, h, n, d)

    def rs_total(stage, h, n):
        for side in range(2):
            arrived(
                nb.at[stage, h, n, side],
                rss.at[stage, h, n, 2 + side],
                rsr.at[stage, h, n, 2 + side],
            )
        return (
            on_chip(stage, h, n, 0) + nb[stage, h, n, 0].astype(F32) + nb[stage, h, n, 1].astype(F32)
        )

    def columns(p):
        return pl.ds(pl.multiple_of(p * bw, bw), bw)

    def cr_start(i):
        for k in range(1, 8):
            p = (t + k) % 8
            remote(
                dpart.at[i, :, columns(p)], drs.at[i, k], crs.at[i, k], crr.at[i, k], (g, p)
            )

    def cr_total(i):
        total = dpart[i, :, columns(t)].astype(F32)
        for k in range(1, 8):
            arrived(drs.at[i, k], crs.at[i, k], crr.at[i, k])
            total = total + drs[i, k].astype(F32)
        return total

    def dp_start(i, block):
        dpb[i, g] = block
        for k in range(1, groups):
            remote(
                dpb.at[i, g], dpb.at[i, g], dps.at[i, k], dpr_sem.at[i, k], ((g + k) % groups, t)
            )

    def dp_total(i):
        for k in range(1, groups):
            source = (g + groups - k) % groups
            arrived(dpb.at[i, source], dps.at[i, k], dpr_sem.at[i, k])
        return dpb[i].reshape(nreq, bw)

    def ca_start(i, block):
        dag[i, :, columns(t)] = block
        for k in range(1, 8):
            mine = dag.at[i, :, columns(t)]
            remote(mine, mine, cas.at[i, k], car.at[i, k], (g, (t + k) % 8))

    def ca_finish(i):
        for k in range(1, 8):
            arrived(dag.at[i, :, columns((t + 8 - k) % 8)], cas.at[i, k], car.at[i, k])

    def rotated(part, cosine, sine):
        return part * cosine + pltpu.roll(part, HD // 2, 1) * sine

    def owner_of(b):
        d = b // 2
        return 2 * ((x + d + (d // 2) * (5 - 2 * d)) % 4) + (c + b % 2) % 2

    part_rows = 8 * SIZE

    def place_of(index):
        b = (index // SIZE) % 8
        d = b >> 1
        owner = 2 * ((x + (d ^ (d >> 1))) & 3) + ((c + (b & 1)) & 1)
        return owner * (BATCHES * SIZE) + SIZE * (index // part_rows) + index % SIZE

    def project(h):
        part = jnp.dot(xg1[h], w_qkv[...], preferred_element_type=F32)
        here = slice(part_rows * h, part_rows * (h + 1))
        there = slice(stored + part_rows * h, stored + part_rows * (h + 1))
        cosine = cos_ref[here, :]
        sine = sin_ref[here, :]
        for head in range(2):
            qb[h, head] = rotated(part[:, HD * head : HD * (head + 1)], cosine, sine).astype(BF16)
        kall[there, :] = rotated(part[:, 2 * HD : 3 * HD], cosine, sine).astype(BF16)
        vall[there, :] = part[:, 3 * HD : 4 * HD].astype(BF16)

    def entries(h):
        for b in range(8):
            first = pl.multiple_of(owner_of(b) * (BATCHES * SIZE) + SIZE * h, SIZE)
            here = pl.ds(stored + part_rows * h + SIZE * b, SIZE)
            pent_ref[0, pl.ds(first, SIZE), :] = kall[here, :]
            pent_ref[1, pl.ds(first, SIZE), :] = vall[here, :]

    def attend(h):
        rows = part_rows
        query = qb[h].reshape(2 * rows, HD)
        scores = lax.dot_general(query, kall[...], NT, preferred_element_type=F32)
        r = lax.broadcasted_iota(jnp.int32, (2 * rows, 1), 0)
        q_place = place_of(rows * h + r % rows)
        k_place = kplace[...]
        scores = jnp.where(k_place <= q_place, scores, NEGATIVE)
        top = jnp.max(scores, axis=-1, keepdims=True)
        weights = jnp.exp2((scores - top) * scale2)
        total = jnp.sum(weights, axis=-1, keepdims=True)
        result = jnp.dot(weights.astype(BF16), vall[...], preferred_element_type=F32)
        result = (result / total).astype(BF16)
        att[h, :, 0:HD] = result[:rows]
        att[h, :, HD : 2 * HD] = result[rows:]

    def out_project(h, n):
        part = jnp.dot(att[h], w_out[:, cw * n : cw * (n + 1)], preferred_element_type=F32)
        rs_split(0, h, n, part)

    def middle(h):
        mine = pl.ds(SIZE * h, SIZE)
        pieces = []
        for n in range(CHUNKS):
            cols = slice(cw * n, cw * (n + 1))
            value = (rows_ref[mine, cols].astype(F32) + rs_total(0, h, n)).astype(BF16)
            resid[mine, cols] = value
            pieces.append(value.astype(F32))
        values = jnp.concatenate(pieces, axis=1)
        xg2[h, 0:SIZE, :] = normed(values, fgain_ref[...])
        ag_start(1, h)

    steps = units // 256

    def gated(h, begin=0, end=steps):
        count = 8 * SIZE + (slots if h == JOINED else 0)
        step = 256

        def one(j, carry):
            cols = pl.ds(pl.multiple_of(j * step, step), step)
            inner = xg2[h, 0:count, :]
            gate_part = jnp.dot(inner, w_gate[:, cols], preferred_element_type=F32)
            up_part = jnp.dot(inner, w_up[:, cols], preferred_element_type=F32)
            hid[0:count, cols] = (
                gate_part / (1.0 + jnp.exp(-gate_part)) * up_part
            ).astype(BF16)
            return carry

        lax.fori_loop(begin, end, one, 0)

    def lower(h, n):
        count = 8 * SIZE + (slots if h == JOINED else 0)
        cols = slice(cw * n, cw * (n + 1))
        part = jnp.dot(hid[0:count, :], w_down[:, cols], preferred_element_type=F32)
        rs_split(1, h, n, part)
        if h == JOINED:
            dpart[2, :, cols] = part[8 * SIZE :].astype(BF16)

    def last(h):
        mine = pl.ds(SIZE * h, SIZE)
        for n in range(CHUNKS):
            cols = slice(cw * n, cw * (n + 1))
            pout_ref[mine, cols] = (resid[mine, cols].astype(F32) + rs_total(1, h, n)).astype(BF16)

    wide = 16 * slots

    def marker(head, flip):
        shape = (slots, wide) if flip else (wide, slots)
        row = lax.broadcasted_iota(jnp.int32, shape, 1 if flip else 0)
        slot = lax.broadcasted_iota(jnp.int32, shape, 0 if flip else 1)
        return (row == 16 * slot + head).astype(F32).astype(BF16)

    def decode_project():
        inner = normed(dag[0].astype(F32), again_ref[...])
        part = jnp.dot(inner, w_qkv[...], preferred_element_type=F32)
        cosine = cos_ref[fresh : fresh + slots, :]
        sine = sin_ref[fresh : fresh + slots, :]
        spread = jnp.zeros((wide, HD), F32)
        for head in range(2):
            query = rotated(part[:, HD * head : HD * (head + 1)], cosine, sine).astype(BF16)
            spread = spread + jnp.dot(marker(head, False), query, preferred_element_type=F32)
        qpad[...] = spread.astype(BF16)
        key = rotated(part[:, 2 * HD : 3 * HD], cosine, sine).astype(BF16)
        value = part[:, 3 * HD : 4 * HD].astype(BF16)
        dent_ref[0] = key
        dent_ref[1] = value
        knew[...] = jnp.zeros_like(knew)
        vnew[...] = jnp.zeros_like(vnew)
        knew[0:slots, :] = key
        vnew[0:slots, :] = value

    def decode_attend(begin, end):
        def score(n, carry):
            here = pl.ds(pl.multiple_of(16 * n, 16), 16)
            part = lax.dot_general(qpad[here, :], kdec[n], NT, preferred_element_type=F32)
            col = lax.broadcasted_iota(jnp.int32, (16, dstored), 1)
            dsc[here, 0:dstored] = jnp.where(col < len_ref[n], part, NEGATIVE)
            return carry

        lax.fori_loop(begin, end, score, 0, unroll=4)

    def decode_weigh():
        own = lax.dot_general(qpad[...], knew[...], NT, preferred_element_type=F32)
        row = lax.broadcasted_iota(jnp.int32, (wide, HD), 0)
        col = lax.broadcasted_iota(jnp.int32, (wide, HD), 1)
        dsc[:, dstored:] = jnp.where(col == (row >> 4), own, NEGATIVE)
        scores = dsc[...]
        top = jnp.max(scores, axis=-1, keepdims=True)
        weights = jnp.exp2((scores - top) * scale2)
        dtotal[...] = jnp.sum(weights, axis=-1, keepdims=True)
        dpr[...] = weights.astype(BF16)

    def decode_mix():
        def mix(n, carry):
            here = pl.ds(pl.multiple_of(16 * n, 16), 16)
            dob[here, :] = jnp.dot(dpr[here, 0:dstored], vdec[n], preferred_element_type=F32)
            return carry

        lax.fori_loop(0, slots, mix, 0, unroll=4)
        result = dob[...] + jnp.dot(dpr[:, dstored:], vnew[...], preferred_element_type=F32)
        result = (result / dtotal[...]).astype(BF16)
        picked = [
            jnp.dot(marker(head, True), result, preferred_element_type=F32).astype(BF16)
            for head in range(2)
        ]
        attended = jnp.concatenate(picked, axis=1)
        dpart[1] = jnp.dot(attended, w_out[...], preferred_element_type=F32).astype(BF16)

    def own_rows(h):
        mine = pl.ds(SIZE * h, SIZE)
        xg1[h, 0:SIZE, :] = normed(rows_ref[mine, :].astype(F32), again_ref[...])

    spot = lax.broadcasted_iota(jnp.int32, (slots, width), 0)

    def own_decode_rows():
        pair = drows_ref[...].astype(F32)
        dpart[0] = (
            jnp.where(spot == 2 * t, pair[0:1], 0.0) + jnp.where(spot == 2 * t + 1, pair[1:2], 0.0)
        ).astype(BF16)

    def tables():
        lane = lax.broadcasted_iota(jnp.int32, (1, HD), 1)
        powers = (lane % (HD // 2)).astype(F32) * (2.0 / HD)
        inverse = jnp.exp(powers * (-math.log(THETA)))
        sign = jnp.where(lane < HD // 2, -1.0, 1.0).astype(F32)

        def table(first, count, places):
            angles = places.astype(F32) * inverse
            cos_ref[pl.ds(first, count), :] = jnp.cos(angles)
            sin_ref[pl.ds(first, count), :] = jnp.sin(angles) * sign

        def some(i, carry):
            row = lax.broadcasted_iota(jnp.int32, (64, HD), 0)
            table(pl.multiple_of(64 * i, 64), 64, off_ref[0] + place_of(64 * i + row))
            return carry

        lax.fori_loop(0, fresh // 64, some, 0)
        col = lax.broadcasted_iota(jnp.int32, (1, stored + fresh), 1)
        kplace[...] = jnp.where(
            col < stored,
            jnp.where(col < off_ref[0], -1, fresh),
            place_of(jnp.maximum(col - stored, 0)),
        )
        slot = lax.broadcasted_iota(jnp.int32, (slots, HD), 0)
        length = jnp.zeros((slots, HD), jnp.int32)
        for n in range(slots):
            length = jnp.where(slot == n, len_ref[n], length)
        table(fresh, slots, length)

    member = lax.broadcasted_iota(jnp.int32, (slots, nreq), 0) + slots * g
    listed = lax.broadcasted_iota(jnp.int32, (slots, nreq), 1)

    def choices():
        request = lax.broadcasted_iota(jnp.int32, (nreq, nreq), 0)
        holder = (request == deal_ref[...]).astype(F32).astype(BF16)
        picker[...] = lax.dot_general(
            (member == listed).astype(F32).astype(BF16), holder, NT, preferred_element_type=F32
        ).astype(BF16)
        chooser[...] = (member == deal_ref[...]).astype(F32).astype(BF16)

    def first_deal():
        if across:
            pl.semaphore_wait(passed, len(across))
        dp_start(0, cr_total(0).astype(BF16))

    def dealt():
        ca_start(0, jnp.dot(chooser[...], dp_total(0), preferred_element_type=F32).astype(BF16))

    def decode_middle():
        total = dag[0, :, columns(t)].astype(F32) + cr_total(1)
        ca_start(1, total.astype(BF16))

    def decode_inner():
        ca_finish(1)
        xg2[JOINED, part_rows:, :] = normed(dag[1].astype(F32), fgain_ref[...])

    def decode_last():
        total = dag[1, :, columns(t)].astype(F32) + cr_total(2)
        dp_start(1, total.astype(BF16))

    def undealt():
        ca_start(2, jnp.dot(picker[...], dp_total(1), preferred_element_type=F32).astype(BF16))

    def decode_out():
        ca_finish(2)
        every = dag[2].astype(F32)
        first = jnp.sum(jnp.where(spot == 2 * t, every, 0.0), axis=0, keepdims=True)
        second = jnp.sum(jnp.where(spot == 2 * t + 1, every, 0.0), axis=0, keepdims=True)
        dout_ref[...] = jnp.concatenate([first, second], axis=0).astype(BF16)

    own_decode_rows()
    own_rows(0)
    own_rows(1)

    pl.semaphore_wait(barrier, 7 + len(below) + len(across))
    for other in across:
        pl.semaphore_signal(passed, inc=1, device_id=(other, t), device_id_type=MESH)


    ag_start(0, 0)
    ag_start(0, 1)
    own_rows(2)
    ag_start(0, 2)
    own_rows(3)
    ag_start(0, 3)
    tables()
    choices()
    cr_start(0)
    ag_onward(0, 0)
    ag_share(0, 0)
    ag_onward(0, 1)
    ag_share(0, 1)
    ag_onward(0, 2)
    ag_share(0, 2)
    ag_onward(0, 3)
    ag_share(0, 3)
    ag_far(0, 0)
    first_deal()
    ag_far(0, 1)
    local["qkv"].wait()
    ag_finish(0, 0)
    project(0)
    ag_far(0, 2)
    entries(0)
    ag_finish(0, 1)
    project(1)
    ag_far(0, 3)
    entries(1)
    ag_finish(0, 2)
    project(2)
    entries(2)
    ag_finish(0, 3)
    project(3)
    local["pk"].wait()
    local["pv"].wait()
    local["out"].wait()
    attend(0)
    entries(3)
    out_project(0, 0)
    out_project(0, 1)
    attend(1)
    dealt()
    out_project(1, 0)
    out_project(1, 1)
    rs_combine(0, 0)
    attend(2)
    out_project(2, 0)
    out_project(2, 1)
    rs_combine(0, 1)
    attend(3)
    out_project(3, 0)
    out_project(3, 1)
    rs_combine(0, 2)
    rs_relay(0, 0)
    ca_finish(0)
    decode_project()
    local["dk"].wait()
    decode_attend(0, slots // 2)
    rs_relay(0, 1)
    rs_combine(0, 3)
    decode_attend(slots // 2, slots)
    decode_weigh()
    local["dv"].wait()
    decode_mix()
    cr_start(1)
    middle(0)
    rs_relay(0, 2)
    middle(1)
    rs_relay(0, 3)
    ag_onward(1, 0)
    decode_middle()
    ag_share(1, 0)
    middle(2)
    ag_onward(1, 1)
    ag_share(1, 1)
    middle(3)
    ag_far(1, 0)
    ag_onward(1, 2)
    decode_inner()
    local["gate"].wait()
    local["up"].wait()
    local["down"].wait()
    ag_finish(1, 0)
    gated(0, 0, steps // 2)
    ag_share(1, 2)
    gated(0, steps // 2, steps)
    ag_far(1, 1)
    lower(0, 0)
    ag_onward(1, 3)
    lower(0, 1)
    cr_start(2)
    ag_share(1, 3)
    ag_finish(1, 1)
    gated(1, 0, steps // 2)
    ag_far(1, 2)
    gated(1, steps // 2, steps)
    rs_combine(1, 0)
    lower(1, 0)
    lower(1, 1)
    ag_far(1, 3)
    ag_finish(1, 2)
    gated(2, 0, steps // 2)
    gated(2, steps // 2, steps)
    rs_combine(1, 1)
    decode_last()
    lower(2, 0)
    rs_relay(1, 0)
    lower(2, 1)
    ag_finish(1, 3)
    gated(3, 0, steps // 2)
    gated(3, steps // 2, steps)
    rs_combine(1, 2)
    lower(3, 0)
    lower(3, 1)
    rs_relay(1, 1)
    last(0)
    rs_combine(1, 3)
    rs_relay(1, 2)
    undealt()
    last(1)
    rs_relay(1, 3)
    last(2)
    last(3)
    decode_out()

    for copy in sends:
        copy.wait_send()


def hand_out(*refs):
    count = len(refs) // 3 + 1
    sources, targets, sems = refs[:count], refs[count : 2 * count], refs[2 * count]
    copies = [
        pltpu.make_async_copy(source, target, sems.at[i])
        for i, (source, target) in enumerate(zip(sources, targets))
    ]
    for copy in copies:
        copy.start()
    for copy in copies:
        copy.wait()


def on_device(
    groups,
    prefill_rows,
    decode_rows,
    deal_order,
    prefill_offset,
    cache_length,
    prefill_cache,
    decode_cache,
    qkv_weight,
    out_weight,
    attention_gain,
    forward_gain,
    gate_weight,
    up_weight,
    down_weight,
):
    width = prefill_rows.shape[1]
    fresh = 8 * prefill_rows.shape[0]
    slots = cache_length.shape[0]
    stored = prefill_cache.shape[2]
    dstored = decode_cache.shape[2]
    units = gate_weight.shape[1]
    cw = width // CHUNKS
    bw = width // 8
    vmem = pl.BlockSpec(memory_space=pltpu.VMEM)
    smem = pl.BlockSpec(memory_space=pltpu.SMEM)
    hbm = pl.BlockSpec(memory_space=pl.ANY)
    dma = pltpu.SemaphoreType.DMA
    shape = jax.ShapeDtypeStruct
    results = pl.pallas_call(
        functools.partial(layer_kernel, groups),
        name="layer",
        out_shape=(
            shape(prefill_rows.shape, BF16),
            shape(decode_rows.shape, BF16),
            shape((2, fresh, HD), BF16),
            shape((2, slots, HD), BF16),
        ),
        in_specs=[vmem, vmem, vmem, smem, smem, vmem, vmem] + [hbm] * 7,
        out_specs=(vmem, vmem, vmem, vmem),
        scratch_shapes=[
            pltpu.VMEM((width, 4 * HD), BF16),
            pltpu.VMEM((2 * HD, width), BF16),
            pltpu.VMEM((width, units), BF16),
            pltpu.VMEM((width, units), BF16),
            pltpu.VMEM((units, width), BF16),
            pltpu.VMEM((stored + fresh, HD), BF16),
            pltpu.VMEM((stored + fresh, HD), BF16),
            pltpu.VMEM((slots, dstored, HD), BF16),
            pltpu.VMEM((slots, dstored, HD), BF16),
            pltpu.VMEM((BATCHES, 8 * SIZE, width), BF16),
            pltpu.VMEM((BATCHES, 8 * SIZE + slots, width), BF16),
            pltpu.VMEM((1, stored + fresh), jnp.int32),
            pltpu.VMEM((slots, groups * slots), BF16),
            pltpu.VMEM((slots, groups * slots), BF16),
            pltpu.VMEM((16 * slots, 1), F32),
            pltpu.VMEM((BATCHES, 2, 8 * SIZE, HD), BF16),
            pltpu.VMEM((BATCHES, 8 * SIZE, 2 * HD), BF16),
            pltpu.VMEM((2, BATCHES, CHUNKS, 2, 4, SIZE, cw), BF16),
            pltpu.VMEM((2, BATCHES, CHUNKS, 4, SIZE, cw), BF16),
            pltpu.VMEM((2, BATCHES, CHUNKS, 4, SIZE, cw), BF16),
            pltpu.VMEM((2, BATCHES, CHUNKS, SIZE, cw), BF16),
            pltpu.VMEM((2, BATCHES, CHUNKS, 2, SIZE, cw), BF16),
            pltpu.VMEM(prefill_rows.shape, BF16),
            pltpu.VMEM((8 * SIZE + slots, units), BF16),
            pltpu.VMEM((3, slots, width), BF16),
            pltpu.VMEM((3, 8, slots, bw), BF16),
            pltpu.VMEM((2, groups, slots, bw), BF16),
            pltpu.VMEM((3, slots, width), BF16),
            pltpu.VMEM((16 * slots, dstored + HD), F32),
            pltpu.VMEM((16 * slots, dstored + HD), BF16),
            pltpu.VMEM((16 * slots, HD), BF16),
            pltpu.VMEM((HD, HD), BF16),
            pltpu.VMEM((HD, HD), BF16),
            pltpu.VMEM((16 * slots, HD), F32),
            pltpu.VMEM((fresh + slots, HD), F32),
            pltpu.VMEM((fresh + slots, HD), F32),
            dma((9,)),
            dma((2, BATCHES, 10)),
            dma((2, BATCHES, 10)),
            dma((2, BATCHES, CHUNKS, 4)),
            dma((2, BATCHES, CHUNKS, 4)),
            dma((3, 8)),
            dma((3, 8)),
            dma((2, groups)),
            dma((2, groups)),
            dma((3, 8)),
            dma((3, 8)),
            pltpu.SemaphoreType.REGULAR,
        ],
        compiler_params=pltpu.CompilerParams(
            collective_id=0, has_side_effects=True, vmem_limit_bytes=66_000_000
        ),
    )(
        prefill_rows,
        decode_rows,
        deal_order[None, :],
        prefill_offset,
        cache_length,
        attention_gain[None, :],
        forward_gain[None, :],
        prefill_cache,
        decode_cache,
        qkv_weight.reshape(width, 4 * HD),
        out_weight,
        gate_weight,
        up_weight,
        down_weight,
    )
    return pl.pallas_call(
        hand_out,
        name="hand_out",
        out_shape=tuple(shape(result.shape, BF16) for result in results),
        in_specs=[vmem] * 4,
        out_specs=(hbm,) * 4,
        scratch_shapes=[dma((4,))],
    )(*results)


def solution(mesh):
    placed = (
        P(("dp", "tensor"), None),
        P(("dp", "tensor"), None),
        P(),
        P("dp"),
        P("dp"),
        P(None, "dp", None, "tensor"),
        P(None, "dp", None, "tensor"),
        P(None, "tensor", None),
        P("tensor", None),
        P(),
        P(),
        P(None, "tensor"),
        P(None, "tensor"),
        P("tensor", None),
    )
    return jax.shard_map(
        functools.partial(on_device, mesh.shape["dp"]),
        mesh=mesh,
        in_specs=placed,
        out_specs=(
            P(("dp", "tensor"), None),
            P(("dp", "tensor"), None),
            P(None, "dp", "tensor"),
            P(None, "dp", "tensor"),
        ),
        check_vma=False,
    )
```

```python
import functools
import math

import jax
import jax.numpy as jnp
from jax import lax
from jax.experimental import pallas as pl
from jax.experimental.pallas import tpu as pltpu
from jax.sharding import PartitionSpec as P

HD = 128
EPSILON = 1e-06
THETA = 1000000.0
NEGATIVE = -1e30
MESH = pl.DeviceIdType.MESH
F32 = jnp.float32
BF16 = jnp.bfloat16
NT = (((1,), (1,)), ((), ()))
BATCHES = 4
SIZE = 16
JOINED = 0
GATHER_DIRECT = ()
SCATTER_DIRECT = ()
CHUNKS = 2


def normed(values, gain):
    spread = jnp.mean(values * values, axis=-1, keepdims=True)
    return (values * lax.rsqrt(spread + EPSILON) * gain).astype(BF16)


def layer_kernel(
    groups,
    rows_hbm,
    drows_hbm,
    deal_hbm,
    off_hbm,
    len_hbm,
    again_hbm,
    fgain_hbm,
    pcache,
    dcache,
    qkv_hbm,
    out_hbm,
    gate_hbm,
    up_hbm,
    down_hbm,
    pout_hbm,
    dout_hbm,
    pent_hbm,
    dent_hbm,
    w_qkv,
    w_out,
    w_gate,
    w_up,
    w_down,
    kall,
    vall,
    kdec,
    vdec,
    xg1,
    xg2,
    kplace,
    picker,
    chooser,
    dtotal,
    qb,
    att,
    pb,
    rcv,
    cb,
    fb,
    nb,
    resid,
    hid,
    dpart,
    drs,
    dpb,
    dag,
    dsc,
    dpr,
    qpad,
    knew,
    vnew,
    dob,
    cos_ref,
    sin_ref,
    wsem,
    ags,
    agr,
    rss,
    rsr,
    crs,
    crr,
    dps,
    dpr_sem,
    cas,
    car,
    passed,
    rows_ref,
    drows_ref,
    deal_ref,
    off_ref,
    len_ref,
    again_ref,
    fgain_ref,
    pout_ref,
    dout_ref,
    pent_ref,
    dent_ref,
    osem,
):
    g = lax.axis_index("dp")
    t = lax.axis_index("tensor")
    x = t // 2
    c = t % 2
    width = rows_hbm.shape[1]
    cw = width // CHUNKS
    bw = width // 8
    stored = pcache.shape[2]
    fresh = pent_hbm.shape[1]
    slots = dent_hbm.shape[1]
    dstored = dcache.shape[2]
    units = w_gate.shape[1]
    nreq = groups * slots
    scale2 = (1.0 / math.sqrt(HD)) * math.log2(math.e)

    partner = (g, t + 1 - 2 * c)
    right = (g, ((x + 1) % 4) * 2 + c)
    left = (g, ((x + 3) % 4) * 2 + c)
    far = (g, ((x + 2) % 4) * 2 + c)
    sends = []

    def remote(src, dst, ss, rs, dev):
        copy = pltpu.make_async_remote_copy(
            src_ref=src, dst_ref=dst, send_sem=ss, recv_sem=rs, device_id=dev, device_id_type=MESH
        )
        copy.start()
        sends.append(copy)

    def arrived(dst, ss, rs):
        pltpu.make_async_remote_copy(
            src_ref=dst, dst_ref=dst, send_sem=ss, recv_sem=rs, device_id=partner, device_id_type=MESH
        ).wait_recv()

    deep = min(4, groups)
    high = groups // deep
    below = [(g // deep) * deep + (g + k) % deep for k in range(1, deep)]
    across = [(g + deep * k) % groups for k in range(1, high)]
    barrier = pltpu.get_barrier_semaphore()
    for k in range(1, 8):
        pl.semaphore_signal(barrier, inc=1, device_id=(g, (t + k) % 8), device_id_type=MESH)
    for other in below + across:
        pl.semaphore_signal(barrier, inc=1, device_id=(other, t), device_id_type=MESH)

    local = {}

    def fetch(name, src, dst):
        copy = pltpu.make_async_copy(src, dst, wsem.at[len(local)])
        copy.start()
        local[name] = copy

    fetch("rows", rows_hbm, rows_ref)
    fetch("drows", drows_hbm, drows_ref)
    fetch("again", again_hbm, again_ref)
    fetch("off", off_hbm, off_ref)
    fetch("len", len_hbm, len_ref)
    fetch("deal", deal_hbm, deal_ref)
    fetch("fgain", fgain_hbm, fgain_ref)
    fetch("qkv", qkv_hbm, w_qkv)
    fetch("pk", pcache.at[0, 0], kall.at[pl.ds(0, stored)])
    fetch("pv", pcache.at[1, 0], vall.at[pl.ds(0, stored)])
    fetch("out", out_hbm, w_out)
    fetch("dk", dcache.at[0], kdec)
    fetch("dv", dcache.at[1], vdec)
    fetch("gate", gate_hbm, w_gate)
    fetch("up", up_hbm, w_up)
    fetch("down", down_hbm, w_down)

    handed = []

    def hand(source, target):
        copy = pltpu.make_async_copy(source, target, osem.at[len(handed)])
        copy.start()
        handed.append(copy)

    def buffer_of(stage, h):
        return (xg1 if stage == 0 else xg2).at[h]

    def ag_block(stage, h, b, p):
        rows = pl.ds(SIZE * b, SIZE)
        if p is None:
            return buffer_of(stage, h).at[rows]
        return buffer_of(stage, h).at[rows, pl.ds(width // 2 * p, width // 2)]

    def ag_send(stage, h, src_b, dst_b, p, number, dev):
        remote(
            ag_block(stage, h, src_b, p),
            ag_block(stage, h, dst_b, p),
            ags.at[stage, h, number],
            agr.at[stage, h, number],
            dev,
        )

    def ag_wait(stage, h, b, p, number):
        arrived(ag_block(stage, h, b, p), ags.at[stage, h, number], agr.at[stage, h, number])

    def ag_start(stage, h):
        if (stage, h) in GATHER_DIRECT:
            ag_send(stage, h, 0, 6, None, 5, far)
        ag_send(stage, h, 0, 4, 0, 1, right)
        ag_send(stage, h, 0, 2, 1, 4, left)
        ag_send(stage, h, 0, 4, 1, 2, right)
        ag_send(stage, h, 0, 2, 0, 3, left)
        ag_send(stage, h, 0, 1, None, 0, partner)

    def ag_onward(stage, h):
        if (stage, h) in GATHER_DIRECT:
            return
        ag_wait(stage, h, 4, 0, 1)
        ag_send(stage, h, 4, 6, 0, 5, right)
        ag_wait(stage, h, 2, 1, 4)
        ag_send(stage, h, 2, 6, 1, 6, left)

    def ag_share(stage, h):
        if (stage, h) in GATHER_DIRECT:
            ag_wait(stage, h, 4, 0, 1)
            ag_wait(stage, h, 2, 1, 4)
        ag_wait(stage, h, 4, 1, 2)
        ag_send(stage, h, 4, 5, None, 7, partner)
        ag_wait(stage, h, 2, 0, 3)
        ag_send(stage, h, 2, 3, None, 8, partner)

    def ag_far(stage, h):
        if (stage, h) in GATHER_DIRECT:
            ag_wait(stage, h, 6, None, 5)
        else:
            ag_wait(stage, h, 6, 0, 5)
            ag_wait(stage, h, 6, 1, 6)
        ag_send(stage, h, 6, 7, None, 9, partner)

    def ag_finish(stage, h):
        for b, number in ((1, 0), (5, 7), (3, 8), (7, 9)):
            ag_wait(stage, h, b, None, number)

    def rs_split(stage, h, n, part):
        for b in range(8):
            pb[stage, h, n, b % 2, b // 2] = part[SIZE * b : SIZE * (b + 1)].astype(BF16)
        remote(
            pb.at[stage, h, n, 1],
            rcv.at[stage, h, n],
            rss.at[stage, h, n, 0],
            rsr.at[stage, h, n, 0],
            partner,
        )

    def on_chip(stage, h, n, d):
        return pb[stage, h, n, 0, d].astype(F32) + rcv[stage, h, n, d].astype(F32)

    def to_side(stage, h, n, d):
        side, dev = (0, right) if d == 1 else (1, left)
        remote(
            cb.at[stage, h, n, d],
            nb.at[stage, h, n, side],
            rss.at[stage, h, n, 2 + side],
            rsr.at[stage, h, n, 2 + side],
            dev,
        )

    def rs_combine(stage, h):
        for n in range(CHUNKS):
            arrived(rcv.at[stage, h, n], rss.at[stage, h, n, 0], rsr.at[stage, h, n, 0])
            cb[stage, h, n, 3] = on_chip(stage, h, n, 3).astype(BF16)
            remote(
                cb.at[stage, h, n, 3],
                fb.at[stage, h, n],
                rss.at[stage, h, n, 1],
                rsr.at[stage, h, n, 1],
                far if (stage, h) in SCATTER_DIRECT else right if n % 2 == 0 else left,
            )
        for n in range(CHUNKS):
            first = 2 if n % 2 == 0 else 1
            for d in (first, 3 - first) if (stage, h) in SCATTER_DIRECT else (first,):
                cb[stage, h, n, d] = on_chip(stage, h, n, d).astype(BF16)
                to_side(stage, h, n, d)

    def rs_relay(stage, h):
        if (stage, h) in SCATTER_DIRECT:
            return
        for n in range(CHUNKS):
            rs_relay_chunk(stage, h, n)

    def rs_relay_chunk(stage, h, n):
        arrived(fb.at[stage, h, n], rss.at[stage, h, n, 1], rsr.at[stage, h, n, 1])
        d = 1 if n % 2 == 0 else 2
        cb[stage, h, n, d] = (on_chip(stage, h, n, d) + fb[stage, h, n].astype(F32)).astype(BF16)
        to_side(stage, h, n, d)

    def rs_total(stage, h, n):
        for side in range(2):
            arrived(
                nb.at[stage, h, n, side],
                rss.at[stage, h, n, 2 + side],
                rsr.at[stage, h, n, 2 + side],
            )
        total = on_chip(stage, h, n, 0) + nb[stage, h, n, 0].astype(F32) + nb[stage, h, n, 1].astype(F32)
        if (stage, h) in SCATTER_DIRECT:
            arrived(fb.at[stage, h, n], rss.at[stage, h, n, 1], rsr.at[stage, h, n, 1])
            total = total + fb[stage, h, n].astype(F32)
        return total

    def columns(p):
        return pl.ds(pl.multiple_of(p * bw, bw), bw)

    def cr_start(i):
        for k in range(1, 8):
            p = (t + k) % 8
            remote(
                dpart.at[i, :, columns(p)], drs.at[i, k], crs.at[i, k], crr.at[i, k], (g, p)
            )

    def cr_total(i):
        total = dpart[i, :, columns(t)].astype(F32)
        for k in range(1, 8):
            arrived(drs.at[i, k], crs.at[i, k], crr.at[i, k])
            total = total + drs[i, k].astype(F32)
        return total

    def dp_start(i, block):
        dpb[i, g] = block
        for k in range(1, groups):
            remote(
                dpb.at[i, g], dpb.at[i, g], dps.at[i, k], dpr_sem.at[i, k], ((g + k) % groups, t)
            )

    def dp_total(i):
        for k in range(1, groups):
            source = (g + groups - k) % groups
            arrived(dpb.at[i, source], dps.at[i, k], dpr_sem.at[i, k])
        return dpb[i].reshape(nreq, bw)

    def ca_start(i, block):
        dag[i, :, columns(t)] = block
        for k in range(1, 8):
            mine = dag.at[i, :, columns(t)]
            remote(mine, mine, cas.at[i, k], car.at[i, k], (g, (t + k) % 8))

    def ca_finish(i):
        for k in range(1, 8):
            arrived(dag.at[i, :, columns((t + 8 - k) % 8)], cas.at[i, k], car.at[i, k])

    def rotated(part, cosine, sine):
        return part * cosine + pltpu.roll(part, HD // 2, 1) * sine

    def owner_of(b):
        d = b // 2
        return 2 * ((x + d + (d // 2) * (5 - 2 * d)) % 4) + (c + b % 2) % 2

    part_rows = 8 * SIZE

    def place_of(index):
        b = (index // SIZE) % 8
        d = b >> 1
        owner = 2 * ((x + (d ^ (d >> 1))) & 3) + ((c + (b & 1)) & 1)
        return owner * (BATCHES * SIZE) + SIZE * (index // part_rows) + index % SIZE

    def project(h):
        part = jnp.dot(xg1[h], w_qkv[...], preferred_element_type=F32)
        here = slice(part_rows * h, part_rows * (h + 1))
        there = slice(stored + part_rows * h, stored + part_rows * (h + 1))
        cosine = cos_ref[here, :]
        sine = sin_ref[here, :]
        for head in range(2):
            qb[h, head] = rotated(part[:, HD * head : HD * (head + 1)], cosine, sine).astype(BF16)
        kall[there, :] = rotated(part[:, 2 * HD : 3 * HD], cosine, sine).astype(BF16)
        vall[there, :] = part[:, 3 * HD : 4 * HD].astype(BF16)

    entered = []

    def entries(h):
        for b in range(8):
            first = pl.multiple_of(owner_of(b) * (BATCHES * SIZE) + SIZE * h, SIZE)
            here = pl.ds(stored + part_rows * h + SIZE * b, SIZE)
            pent_ref[0, pl.ds(first, SIZE), :] = kall[here, :]
            pent_ref[1, pl.ds(first, SIZE), :] = vall[here, :]
        entered.append(h)
        if len(entered) == BATCHES:
            hand(pent_ref, pent_hbm)

    def attend(h):
        rows = part_rows
        query = qb[h].reshape(2 * rows, HD)
        scores = lax.dot_general(query, kall[...], NT, preferred_element_type=F32)
        r = lax.broadcasted_iota(jnp.int32, (2 * rows, 1), 0)
        q_place = place_of(rows * h + r % rows)
        k_place = kplace[...]
        scores = jnp.where(k_place <= q_place, scores, NEGATIVE)
        top = jnp.max(scores, axis=-1, keepdims=True)
        weights = jnp.exp2((scores - top) * scale2)
        total = jnp.sum(weights, axis=-1, keepdims=True)
        result = jnp.dot(weights.astype(BF16), vall[...], preferred_element_type=F32)
        result = (result / total).astype(BF16)
        att[h, :, 0:HD] = result[:rows]
        att[h, :, HD : 2 * HD] = result[rows:]

    def out_project(h, n):
        part = jnp.dot(att[h], w_out[:, cw * n : cw * (n + 1)], preferred_element_type=F32)
        rs_split(0, h, n, part)

    def middle(h):
        mine = pl.ds(SIZE * h, SIZE)
        pieces = []
        for n in range(CHUNKS):
            cols = slice(cw * n, cw * (n + 1))
            value = (rows_ref[mine, cols].astype(F32) + rs_total(0, h, n)).astype(BF16)
            resid[mine, cols] = value
            pieces.append(value.astype(F32))
        values = jnp.concatenate(pieces, axis=1)
        xg2[h, 0:SIZE, :] = normed(values, fgain_ref[...])
        ag_start(1, h)

    steps = units // 256

    def gated(h, begin=0, end=steps):
        count = 8 * SIZE + (slots if h == JOINED else 0)
        step = 256

        def one(j, carry):
            cols = pl.ds(pl.multiple_of(j * step, step), step)
            inner = xg2[h, 0:count, :]
            gate_part = jnp.dot(inner, w_gate[:, cols], preferred_element_type=F32)
            up_part = jnp.dot(inner, w_up[:, cols], preferred_element_type=F32)
            hid[0:count, cols] = (
                gate_part / (1.0 + jnp.exp(-gate_part)) * up_part
            ).astype(BF16)
            return carry

        lax.fori_loop(begin, end, one, 0)

    def lower(h, n):
        count = 8 * SIZE + (slots if h == JOINED else 0)
        cols = slice(cw * n, cw * (n + 1))
        part = jnp.dot(hid[0:count, :], w_down[:, cols], preferred_element_type=F32)
        rs_split(1, h, n, part)
        if h == JOINED:
            dpart[2, :, cols] = part[8 * SIZE :].astype(BF16)

    def last(h):
        mine = pl.ds(SIZE * h, SIZE)
        for n in range(CHUNKS):
            cols = slice(cw * n, cw * (n + 1))
            pout_ref[mine, cols] = (resid[mine, cols].astype(F32) + rs_total(1, h, n)).astype(BF16)
        hand(pout_ref.at[mine], pout_hbm.at[mine])

    wide = 16 * slots

    def marker(head, flip):
        shape = (slots, wide) if flip else (wide, slots)
        row = lax.broadcasted_iota(jnp.int32, shape, 1 if flip else 0)
        slot = lax.broadcasted_iota(jnp.int32, shape, 0 if flip else 1)
        return (row == 16 * slot + head).astype(F32).astype(BF16)

    def decode_project():
        inner = normed(dag[0].astype(F32), again_ref[...])
        part = jnp.dot(inner, w_qkv[...], preferred_element_type=F32)
        cosine = cos_ref[fresh : fresh + slots, :]
        sine = sin_ref[fresh : fresh + slots, :]
        spread = jnp.zeros((wide, HD), F32)
        for head in range(2):
            query = rotated(part[:, HD * head : HD * (head + 1)], cosine, sine).astype(BF16)
            spread = spread + jnp.dot(marker(head, False), query, preferred_element_type=F32)
        qpad[...] = spread.astype(BF16)
        key = rotated(part[:, 2 * HD : 3 * HD], cosine, sine).astype(BF16)
        value = part[:, 3 * HD : 4 * HD].astype(BF16)
        dent_ref[0] = key
        dent_ref[1] = value
        hand(dent_ref, dent_hbm)
        knew[...] = jnp.zeros_like(knew)
        vnew[...] = jnp.zeros_like(vnew)
        knew[0:slots, :] = key
        vnew[0:slots, :] = value

    def decode_attend(begin, end):
        def score(n, carry):
            here = pl.ds(pl.multiple_of(16 * n, 16), 16)
            part = lax.dot_general(qpad[here, :], kdec[n], NT, preferred_element_type=F32)
            col = lax.broadcasted_iota(jnp.int32, (16, dstored), 1)
            dsc[here, 0:dstored] = jnp.where(col < len_ref[n], part, NEGATIVE)
            return carry

        lax.fori_loop(begin, end, score, 0, unroll=4)

    def decode_weigh():
        own = lax.dot_general(qpad[...], knew[...], NT, preferred_element_type=F32)
        row = lax.broadcasted_iota(jnp.int32, (wide, HD), 0)
        col = lax.broadcasted_iota(jnp.int32, (wide, HD), 1)
        dsc[:, dstored:] = jnp.where(col == (row >> 4), own, NEGATIVE)
        scores = dsc[...]
        top = jnp.max(scores, axis=-1, keepdims=True)
        weights = jnp.exp2((scores - top) * scale2)
        dtotal[...] = jnp.sum(weights, axis=-1, keepdims=True)
        dpr[...] = weights.astype(BF16)

    def decode_mix(begin, end):
        def mix(n, carry):
            here = pl.ds(pl.multiple_of(16 * n, 16), 16)
            dob[here, :] = jnp.dot(dpr[here, 0:dstored], vdec[n], preferred_element_type=F32)
            return carry

        lax.fori_loop(begin, end, mix, 0, unroll=4)
    def decode_finish():
        result = dob[...] + jnp.dot(dpr[:, dstored:], vnew[...], preferred_element_type=F32)
        result = (result / dtotal[...]).astype(BF16)
        picked = [
            jnp.dot(marker(head, True), result, preferred_element_type=F32).astype(BF16)
            for head in range(2)
        ]
        attended = jnp.concatenate(picked, axis=1)
        dpart[1] = jnp.dot(attended, w_out[...], preferred_element_type=F32).astype(BF16)

    def own_rows(h):
        mine = pl.ds(SIZE * h, SIZE)
        xg1[h, 0:SIZE, :] = normed(rows_ref[mine, :].astype(F32), again_ref[...])

    spot = lax.broadcasted_iota(jnp.int32, (slots, width), 0)

    def own_decode_rows():
        pair = drows_ref[...].astype(F32)
        dpart[0] = (
            jnp.where(spot == 2 * t, pair[0:1], 0.0) + jnp.where(spot == 2 * t + 1, pair[1:2], 0.0)
        ).astype(BF16)

    def tables():
        lane = lax.broadcasted_iota(jnp.int32, (1, HD), 1)
        powers = (lane % (HD // 2)).astype(F32) * (2.0 / HD)
        inverse = jnp.exp(powers * (-math.log(THETA)))
        sign = jnp.where(lane < HD // 2, -1.0, 1.0).astype(F32)

        def table(first, count, places):
            angles = places.astype(F32) * inverse
            cos_ref[pl.ds(first, count), :] = jnp.cos(angles)
            sin_ref[pl.ds(first, count), :] = jnp.sin(angles) * sign

        def some(i, carry):
            row = lax.broadcasted_iota(jnp.int32, (64, HD), 0)
            table(pl.multiple_of(64 * i, 64), 64, off_ref[0] + place_of(64 * i + row))
            return carry

        lax.fori_loop(0, fresh // 64, some, 0)
        col = lax.broadcasted_iota(jnp.int32, (1, stored + fresh), 1)
        kplace[...] = jnp.where(
            col < stored,
            jnp.where(col < off_ref[0], -1, fresh),
            place_of(jnp.maximum(col - stored, 0)),
        )
        slot = lax.broadcasted_iota(jnp.int32, (slots, HD), 0)
        length = jnp.zeros((slots, HD), jnp.int32)
        for n in range(slots):
            length = jnp.where(slot == n, len_ref[n], length)
        table(fresh, slots, length)

    member = lax.broadcasted_iota(jnp.int32, (slots, nreq), 0) + slots * g
    listed = lax.broadcasted_iota(jnp.int32, (slots, nreq), 1)

    def choices():
        request = lax.broadcasted_iota(jnp.int32, (nreq, nreq), 0)
        holder = (request == deal_ref[...]).astype(F32).astype(BF16)
        picker[...] = lax.dot_general(
            (member == listed).astype(F32).astype(BF16), holder, NT, preferred_element_type=F32
        ).astype(BF16)
        chooser[...] = (member == deal_ref[...]).astype(F32).astype(BF16)

    def first_deal():
        if across:
            pl.semaphore_wait(passed, len(across))
        dp_start(0, cr_total(0).astype(BF16))

    def dealt():
        ca_start(0, jnp.dot(chooser[...], dp_total(0), preferred_element_type=F32).astype(BF16))

    def decode_middle():
        total = dag[0, :, columns(t)].astype(F32) + cr_total(1)
        ca_start(1, total.astype(BF16))

    def decode_inner():
        ca_finish(1)
        xg2[JOINED, part_rows:, :] = normed(dag[1].astype(F32), fgain_ref[...])

    def decode_last():
        total = dag[1, :, columns(t)].astype(F32) + cr_total(2)
        dp_start(1, total.astype(BF16))

    def undealt():
        ca_start(2, jnp.dot(picker[...], dp_total(1), preferred_element_type=F32).astype(BF16))

    def decode_out():
        ca_finish(2)
        every = dag[2].astype(F32)
        first = jnp.sum(jnp.where(spot == 2 * t, every, 0.0), axis=0, keepdims=True)
        second = jnp.sum(jnp.where(spot == 2 * t + 1, every, 0.0), axis=0, keepdims=True)
        dout_ref[...] = jnp.concatenate([first, second], axis=0).astype(BF16)
        hand(dout_ref, dout_hbm)

    for name in ("rows", "drows", "again", "off", "len", "deal", "fgain"):
        local[name].wait()
    own_decode_rows()
    own_rows(0)
    own_rows(1)

    pl.semaphore_wait(barrier, 7 + len(below) + len(across))
    for other in across:
        pl.semaphore_signal(passed, inc=1, device_id=(other, t), device_id_type=MESH)


    cr_start(0)
    ag_start(0, 0)
    ag_start(0, 1)
    own_rows(2)
    ag_start(0, 2)
    own_rows(3)
    ag_start(0, 3)
    tables()
    choices()
    ag_onward(0, 0)
    first_deal()
    ag_share(0, 0)
    ag_onward(0, 1)
    ag_share(0, 1)
    ag_onward(0, 2)
    ag_share(0, 2)
    ag_onward(0, 3)
    ag_share(0, 3)
    ag_far(0, 0)
    ag_far(0, 1)
    dealt()
    local["qkv"].wait()
    ag_finish(0, 0)
    project(0)
    ag_far(0, 2)
    entries(0)
    ag_finish(0, 1)
    project(1)
    ag_far(0, 3)
    entries(1)
    ag_finish(0, 2)
    project(2)
    entries(2)
    ag_finish(0, 3)
    project(3)
    local["pk"].wait()
    local["pv"].wait()
    local["out"].wait()
    attend(0)
    out_project(0, 0)
    out_project(0, 1)
    attend(1)
    out_project(1, 0)
    out_project(1, 1)
    entries(3)
    rs_combine(0, 0)
    attend(2)
    out_project(2, 0)
    ca_finish(0)
    decode_project()
    rs_combine(0, 1)
    local["dk"].wait()
    decode_attend(0, slots // 2)
    out_project(2, 1)
    attend(3)
    rs_relay(0, 0)
    out_project(3, 0)
    out_project(3, 1)
    rs_combine(0, 2)
    decode_attend(slots // 2, slots)
    decode_weigh()
    rs_relay(0, 1)
    local["dv"].wait()
    decode_mix(0, slots // 2)
    rs_combine(0, 3)
    decode_mix(slots // 2, slots)
    decode_finish()
    cr_start(1)
    middle(0)
    rs_relay(0, 2)
    middle(1)
    rs_relay(0, 3)
    ag_onward(1, 0)
    decode_middle()
    ag_share(1, 0)
    middle(2)
    ag_onward(1, 1)
    ag_share(1, 1)
    middle(3)
    ag_far(1, 0)
    ag_onward(1, 2)
    decode_inner()
    local["gate"].wait()
    local["up"].wait()
    local["down"].wait()
    ag_finish(1, 0)
    gated(0, 0, steps // 2)
    gated(0, steps // 2, steps)
    ag_far(1, 1)
    lower(0, 0)
    ag_onward(1, 3)
    ag_share(1, 2)
    lower(0, 1)
    cr_start(2)
    ag_share(1, 3)
    ag_finish(1, 1)
    gated(1, 0, steps // 2)
    ag_far(1, 2)
    gated(1, steps // 2, steps)
    rs_combine(1, 0)
    lower(1, 0)
    lower(1, 1)
    ag_finish(1, 2)
    gated(2, 0, steps // 2)
    ag_far(1, 3)
    gated(2, steps // 2, steps)
    lower(2, 0)
    rs_combine(1, 1)
    decode_last()
    lower(2, 1)
    ag_finish(1, 3)
    gated(3, 0, steps // 2)
    rs_relay(1, 0)
    gated(3, steps // 2, steps)
    rs_combine(1, 2)
    lower(3, 0)
    lower(3, 1)
    rs_relay(1, 1)
    rs_combine(1, 3)
    last(0)
    rs_relay(1, 2)
    undealt()
    last(1)
    rs_relay(1, 3)
    last(2)
    decode_out()
    last(3)

    for copy in sends:
        copy.wait_send()
    for copy in handed:
        copy.wait()


def hand_out(*refs):
    count = len(refs) // 3 + 1
    sources, targets, sems = refs[:count], refs[count : 2 * count], refs[2 * count]
    copies = [
        pltpu.make_async_copy(source, target, sems.at[i])
        for i, (source, target) in enumerate(zip(sources, targets))
    ]
    for copy in copies:
        copy.start()
    for copy in copies:
        copy.wait()


def on_device(
    groups,
    prefill_rows,
    decode_rows,
    deal_order,
    prefill_offset,
    cache_length,
    prefill_cache,
    decode_cache,
    qkv_weight,
    out_weight,
    attention_gain,
    forward_gain,
    gate_weight,
    up_weight,
    down_weight,
):
    width = prefill_rows.shape[1]
    fresh = 8 * prefill_rows.shape[0]
    slots = cache_length.shape[0]
    stored = prefill_cache.shape[2]
    dstored = decode_cache.shape[2]
    units = gate_weight.shape[1]
    cw = width // CHUNKS
    bw = width // 8
    vmem = pl.BlockSpec(memory_space=pltpu.VMEM)
    hbm = pl.BlockSpec(memory_space=pl.ANY)
    dma = pltpu.SemaphoreType.DMA
    shape = jax.ShapeDtypeStruct
    results = pl.pallas_call(
        functools.partial(layer_kernel, groups),
        name="layer",
        out_shape=(
            shape(prefill_rows.shape, BF16),
            shape(decode_rows.shape, BF16),
            shape((2, fresh, HD), BF16),
            shape((2, slots, HD), BF16),
        ),
        in_specs=[pl.BlockSpec(memory_space=pltpu.HBM)] * 7 + [hbm] * 7,
        out_specs=(hbm,) * 4,
        scratch_shapes=[
            pltpu.VMEM((width, 4 * HD), BF16),
            pltpu.VMEM((2 * HD, width), BF16),
            pltpu.VMEM((width, units), BF16),
            pltpu.VMEM((width, units), BF16),
            pltpu.VMEM((units, width), BF16),
            pltpu.VMEM((stored + fresh, HD), BF16),
            pltpu.VMEM((stored + fresh, HD), BF16),
            pltpu.VMEM((slots, dstored, HD), BF16),
            pltpu.VMEM((slots, dstored, HD), BF16),
            pltpu.VMEM((BATCHES, 8 * SIZE, width), BF16),
            pltpu.VMEM((BATCHES, 8 * SIZE + slots, width), BF16),
            pltpu.VMEM((1, stored + fresh), jnp.int32),
            pltpu.VMEM((slots, groups * slots), BF16),
            pltpu.VMEM((slots, groups * slots), BF16),
            pltpu.VMEM((16 * slots, 1), F32),
            pltpu.VMEM((BATCHES, 2, 8 * SIZE, HD), BF16),
            pltpu.VMEM((BATCHES, 8 * SIZE, 2 * HD), BF16),
            pltpu.VMEM((2, BATCHES, CHUNKS, 2, 4, SIZE, cw), BF16),
            pltpu.VMEM((2, BATCHES, CHUNKS, 4, SIZE, cw), BF16),
            pltpu.VMEM((2, BATCHES, CHUNKS, 4, SIZE, cw), BF16),
            pltpu.VMEM((2, BATCHES, CHUNKS, SIZE, cw), BF16),
            pltpu.VMEM((2, BATCHES, CHUNKS, 2, SIZE, cw), BF16),
            pltpu.VMEM(prefill_rows.shape, BF16),
            pltpu.VMEM((8 * SIZE + slots, units), BF16),
            pltpu.VMEM((3, slots, width), BF16),
            pltpu.VMEM((3, 8, slots, bw), BF16),
            pltpu.VMEM((2, groups, slots, bw), BF16),
            pltpu.VMEM((3, slots, width), BF16),
            pltpu.VMEM((16 * slots, dstored + HD), F32),
            pltpu.VMEM((16 * slots, dstored + HD), BF16),
            pltpu.VMEM((16 * slots, HD), BF16),
            pltpu.VMEM((HD, HD), BF16),
            pltpu.VMEM((HD, HD), BF16),
            pltpu.VMEM((16 * slots, HD), F32),
            pltpu.VMEM((fresh + slots, HD), F32),
            pltpu.VMEM((fresh + slots, HD), F32),
            dma((16,)),
            dma((2, BATCHES, 10)),
            dma((2, BATCHES, 10)),
            dma((2, BATCHES, CHUNKS, 4)),
            dma((2, BATCHES, CHUNKS, 4)),
            dma((3, 8)),
            dma((3, 8)),
            dma((2, groups)),
            dma((2, groups)),
            dma((3, 8)),
            dma((3, 8)),
            pltpu.SemaphoreType.REGULAR,
            pltpu.VMEM(prefill_rows.shape, BF16),
            pltpu.VMEM(decode_rows.shape, BF16),
            pltpu.VMEM((1, groups * slots), jnp.int32),
            pltpu.SMEM((1,), jnp.int32),
            pltpu.SMEM((slots,), jnp.int32),
            pltpu.VMEM((1, width), F32),
            pltpu.VMEM((1, width), F32),
            pltpu.VMEM(prefill_rows.shape, BF16),
            pltpu.VMEM(decode_rows.shape, BF16),
            pltpu.VMEM((2, fresh, HD), BF16),
            pltpu.VMEM((2, slots, HD), BF16),
            dma((8,)),
        ],
        compiler_params=pltpu.CompilerParams(
            collective_id=0, has_side_effects=True, vmem_limit_bytes=66_000_000
        ),
    )(
        prefill_rows,
        decode_rows,
        deal_order[None, :],
        prefill_offset,
        cache_length,
        attention_gain[None, :],
        forward_gain[None, :],
        prefill_cache,
        decode_cache,
        qkv_weight.reshape(width, 4 * HD),
        out_weight,
        gate_weight,
        up_weight,
        down_weight,
    )
    return pl.pallas_call(
        hand_out,
        name="hand_out",
        out_shape=tuple(shape(result.shape, BF16) for result in results),
        in_specs=[vmem] * 4,
        out_specs=(hbm,) * 4,
        scratch_shapes=[dma((4,))],
    )(*results)


def solution(mesh):
    placed = (
        P(("dp", "tensor"), None),
        P(("dp", "tensor"), None),
        P(),
        P("dp"),
        P("dp"),
        P(None, "dp", None, "tensor"),
        P(None, "dp", None, "tensor"),
        P(None, "tensor", None),
        P("tensor", None),
        P(),
        P(),
        P(None, "tensor"),
        P(None, "tensor"),
        P("tensor", None),
    )
    return jax.shard_map(
        functools.partial(on_device, mesh.shape["dp"]),
        mesh=mesh,
        in_specs=placed,
        out_specs=(
            P(("dp", "tensor"), None),
            P(("dp", "tensor"), None),
            P(None, "dp", "tensor"),
            P(None, "dp", "tensor"),
        ),
        check_vma=False,
    )
```

```python
import functools
import math

import jax
import jax.numpy as jnp
from jax import lax
from jax.experimental import pallas as pl
from jax.experimental.pallas import tpu as pltpu
from jax.sharding import PartitionSpec as P

HD = 128
EPSILON = 1e-06
THETA = 1000000.0
NEGATIVE = -1e30
MESH = pl.DeviceIdType.MESH
F32 = jnp.float32
BF16 = jnp.bfloat16
NT = (((1,), (1,)), ((), ()))
BATCHES = 4
SIZE = 16
JOINED = 0
GATHER_DIRECT = ()
SCATTER_DIRECT = ()
CHUNKS = 2


def normed(values, gain):
    spread = jnp.mean(values * values, axis=-1, keepdims=True)
    return (values * lax.rsqrt(spread + EPSILON) * gain).astype(BF16)


def layer_kernel(
    groups,
    rows_hbm,
    drows_hbm,
    deal_hbm,
    off_hbm,
    len_hbm,
    again_hbm,
    fgain_hbm,
    pcache,
    dcache,
    qkv_hbm,
    out_hbm,
    gate_hbm,
    up_hbm,
    down_hbm,
    pout_hbm,
    dout_hbm,
    pent_hbm,
    dent_hbm,
    w_qkv,
    w_out,
    w_gate,
    w_up,
    w_down,
    kall,
    vall,
    kdec,
    vdec,
    xg1,
    xg2,
    kplace,
    picker,
    chooser,
    dtotal,
    qb,
    att,
    pb,
    rcv,
    cb,
    fb,
    nb,
    resid,
    hid,
    dpart,
    drs,
    dpb,
    dag,
    dsc,
    dpr,
    qpad,
    knew,
    vnew,
    dob,
    cos_ref,
    sin_ref,
    wsem,
    ags,
    agr,
    rss,
    rsr,
    crs,
    crr,
    dps,
    dpr_sem,
    cas,
    car,
    passed,
    rows_ref,
    drows_ref,
    deal_ref,
    off_ref,
    len_ref,
    again_ref,
    fgain_ref,
    pout_ref,
    dout_ref,
    pent_ref,
    dent_ref,
    osem,
):
    g = lax.axis_index("dp")
    t = lax.axis_index("tensor")
    x = t // 2
    c = t % 2
    width = rows_hbm.shape[1]
    cw = width // CHUNKS
    bw = width // 8
    stored = pcache.shape[2]
    fresh = pent_hbm.shape[1]
    slots = dent_hbm.shape[1]
    dstored = dcache.shape[2]
    units = w_gate.shape[1]
    nreq = groups * slots
    scale2 = (1.0 / math.sqrt(HD)) * math.log2(math.e)

    partner = (g, t + 1 - 2 * c)
    right = (g, ((x + 1) % 4) * 2 + c)
    left = (g, ((x + 3) % 4) * 2 + c)
    far = (g, ((x + 2) % 4) * 2 + c)
    sends = []

    def remote(src, dst, ss, rs, dev):
        copy = pltpu.make_async_remote_copy(
            src_ref=src, dst_ref=dst, send_sem=ss, recv_sem=rs, device_id=dev, device_id_type=MESH
        )
        copy.start()
        sends.append(copy)

    def arrived(dst, ss, rs):
        pltpu.make_async_remote_copy(
            src_ref=dst, dst_ref=dst, send_sem=ss, recv_sem=rs, device_id=partner, device_id_type=MESH
        ).wait_recv()

    deep = min(4, groups)
    high = groups // deep
    below = [(g // deep) * deep + (g + k) % deep for k in range(1, deep)]
    across = [(g + deep * k) % groups for k in range(1, high)]
    barrier = pltpu.get_barrier_semaphore()
    for k in range(1, 8):
        pl.semaphore_signal(barrier, inc=1, device_id=(g, (t + k) % 8), device_id_type=MESH)
    for other in below + across:
        pl.semaphore_signal(barrier, inc=1, device_id=(other, t), device_id_type=MESH)

    local = {}

    def fetch(name, src, dst):
        copy = pltpu.make_async_copy(src, dst, wsem.at[len(local)])
        copy.start()
        local[name] = copy

    fetch("rows", rows_hbm, rows_ref)
    fetch("drows", drows_hbm, drows_ref)
    fetch("again", again_hbm, again_ref)
    fetch("off", off_hbm, off_ref)
    fetch("len", len_hbm, len_ref)
    fetch("deal", deal_hbm, deal_ref)
    fetch("fgain", fgain_hbm, fgain_ref)
    fetch("qkv", qkv_hbm, w_qkv)
    fetch("pk", pcache.at[0, 0], kall.at[pl.ds(0, stored)])
    fetch("pv", pcache.at[1, 0], vall.at[pl.ds(0, stored)])
    fetch("out", out_hbm, w_out)
    fetch("dk", dcache.at[0], kdec)
    fetch("dv", dcache.at[1], vdec)
    fetch("gate", gate_hbm, w_gate)
    fetch("up", up_hbm, w_up)
    fetch("down", down_hbm, w_down)

    handed = []

    def hand(source, target):
        copy = pltpu.make_async_copy(source, target, osem.at[len(handed)])
        copy.start()
        handed.append(copy)

    def buffer_of(stage, h):
        return (xg1 if stage == 0 else xg2).at[h]

    def ag_block(stage, h, b, p):
        rows = pl.ds(SIZE * b, SIZE)
        if p is None:
            return buffer_of(stage, h).at[rows]
        return buffer_of(stage, h).at[rows, pl.ds(width // 2 * p, width // 2)]

    def ag_send(stage, h, src_b, dst_b, p, number, dev):
        remote(
            ag_block(stage, h, src_b, p),
            ag_block(stage, h, dst_b, p),
            ags.at[stage, h, number],
            agr.at[stage, h, number],
            dev,
        )

    def ag_wait(stage, h, b, p, number):
        arrived(ag_block(stage, h, b, p), ags.at[stage, h, number], agr.at[stage, h, number])

    def ag_start(stage, h):
        if (stage, h) in GATHER_DIRECT:
            ag_send(stage, h, 0, 6, None, 5, far)
        ag_send(stage, h, 0, 4, 0, 1, right)
        ag_send(stage, h, 0, 2, 1, 4, left)
        ag_send(stage, h, 0, 4, 1, 2, right)
        ag_send(stage, h, 0, 2, 0, 3, left)
        ag_send(stage, h, 0, 1, None, 0, partner)

    def ag_onward(stage, h):
        if (stage, h) in GATHER_DIRECT:
            return
        ag_wait(stage, h, 4, 0, 1)
        ag_send(stage, h, 4, 6, 0, 5, right)
        ag_wait(stage, h, 2, 1, 4)
        ag_send(stage, h, 2, 6, 1, 6, left)

    def ag_share(stage, h):
        if (stage, h) in GATHER_DIRECT:
            ag_wait(stage, h, 4, 0, 1)
            ag_wait(stage, h, 2, 1, 4)
        ag_wait(stage, h, 4, 1, 2)
        ag_send(stage, h, 4, 5, None, 7, partner)
        ag_wait(stage, h, 2, 0, 3)
        ag_send(stage, h, 2, 3, None, 8, partner)

    def ag_far(stage, h):
        if (stage, h) in GATHER_DIRECT:
            ag_wait(stage, h, 6, None, 5)
        else:
            ag_wait(stage, h, 6, 0, 5)
            ag_wait(stage, h, 6, 1, 6)
        ag_send(stage, h, 6, 7, None, 9, partner)

    def ag_finish(stage, h):
        for b, number in ((1, 0), (5, 7), (3, 8), (7, 9)):
            ag_wait(stage, h, b, None, number)

    def rs_split(stage, h, n, part):
        for b in range(8):
            pb[stage, h, n, b % 2, b // 2] = part[SIZE * b : SIZE * (b + 1)].astype(BF16)
        remote(
            pb.at[stage, h, n, 1],
            rcv.at[stage, h, n],
            rss.at[stage, h, n, 0],
            rsr.at[stage, h, n, 0],
            partner,
        )

    def on_chip(stage, h, n, d):
        return pb[stage, h, n, 0, d].astype(F32) + rcv[stage, h, n, d].astype(F32)

    def to_side(stage, h, n, d):
        side, dev = (0, right) if d == 1 else (1, left)
        remote(
            cb.at[stage, h, n, d],
            nb.at[stage, h, n, side],
            rss.at[stage, h, n, 2 + side],
            rsr.at[stage, h, n, 2 + side],
            dev,
        )

    def rs_combine(stage, h):
        for n in range(CHUNKS):
            arrived(rcv.at[stage, h, n], rss.at[stage, h, n, 0], rsr.at[stage, h, n, 0])
            cb[stage, h, n, 3] = on_chip(stage, h, n, 3).astype(BF16)
            remote(
                cb.at[stage, h, n, 3],
                fb.at[stage, h, n],
                rss.at[stage, h, n, 1],
                rsr.at[stage, h, n, 1],
                far if (stage, h) in SCATTER_DIRECT else right if n % 2 == 0 else left,
            )
        for n in range(CHUNKS):
            first = 2 if n % 2 == 0 else 1
            for d in (first, 3 - first) if (stage, h) in SCATTER_DIRECT else (first,):
                cb[stage, h, n, d] = on_chip(stage, h, n, d).astype(BF16)
                to_side(stage, h, n, d)

    def rs_relay(stage, h):
        if (stage, h) in SCATTER_DIRECT:
            return
        for n in range(CHUNKS):
            rs_relay_chunk(stage, h, n)

    def rs_relay_chunk(stage, h, n):
        arrived(fb.at[stage, h, n], rss.at[stage, h, n, 1], rsr.at[stage, h, n, 1])
        d = 1 if n % 2 == 0 else 2
        cb[stage, h, n, d] = (on_chip(stage, h, n, d) + fb[stage, h, n].astype(F32)).astype(BF16)
        to_side(stage, h, n, d)

    def rs_total(stage, h, n):
        for side in range(2):
            arrived(
                nb.at[stage, h, n, side],
                rss.at[stage, h, n, 2 + side],
                rsr.at[stage, h, n, 2 + side],
            )
        total = on_chip(stage, h, n, 0) + nb[stage, h, n, 0].astype(F32) + nb[stage, h, n, 1].astype(F32)
        if (stage, h) in SCATTER_DIRECT:
            arrived(fb.at[stage, h, n], rss.at[stage, h, n, 1], rsr.at[stage, h, n, 1])
            total = total + fb[stage, h, n].astype(F32)
        return total

    def columns(p):
        return pl.ds(pl.multiple_of(p * bw, bw), bw)

    def cr_start(i):
        for k in range(1, 8):
            p = (t + k) % 8
            remote(
                dpart.at[i, :, columns(p)], drs.at[i, k], crs.at[i, k], crr.at[i, k], (g, p)
            )

    def cr_total(i):
        total = dpart[i, :, columns(t)].astype(F32)
        for k in range(1, 8):
            arrived(drs.at[i, k], crs.at[i, k], crr.at[i, k])
            total = total + drs[i, k].astype(F32)
        return total

    def dp_start(i, block):
        dpb[i, g] = block
        for k in range(1, groups):
            remote(
                dpb.at[i, g], dpb.at[i, g], dps.at[i, k], dpr_sem.at[i, k], ((g + k) % groups, t)
            )

    def dp_total(i):
        for k in range(1, groups):
            source = (g + groups - k) % groups
            arrived(dpb.at[i, source], dps.at[i, k], dpr_sem.at[i, k])
        return dpb[i].reshape(nreq, bw)

    def ca_start(i, block):
        dag[i, :, columns(t)] = block
        for k in range(1, 8):
            mine = dag.at[i, :, columns(t)]
            remote(mine, mine, cas.at[i, k], car.at[i, k], (g, (t + k) % 8))

    def ca_finish(i):
        for k in range(1, 8):
            arrived(dag.at[i, :, columns((t + 8 - k) % 8)], cas.at[i, k], car.at[i, k])

    def rotated(part, cosine, sine):
        return part * cosine + pltpu.roll(part, HD // 2, 1) * sine

    def owner_of(b):
        d = b // 2
        return 2 * ((x + d + (d // 2) * (5 - 2 * d)) % 4) + (c + b % 2) % 2

    part_rows = 8 * SIZE

    def place_of(index):
        b = (index // SIZE) % 8
        d = b >> 1
        owner = 2 * ((x + (d ^ (d >> 1))) & 3) + ((c + (b & 1)) & 1)
        return owner * (BATCHES * SIZE) + SIZE * (index // part_rows) + index % SIZE

    def project(h):
        part = jnp.dot(xg1[h], w_qkv[...], preferred_element_type=F32)
        here = slice(part_rows * h, part_rows * (h + 1))
        there = slice(stored + part_rows * h, stored + part_rows * (h + 1))
        cosine = cos_ref[here, :]
        sine = sin_ref[here, :]
        for head in range(2):
            qb[h, head] = rotated(part[:, HD * head : HD * (head + 1)], cosine, sine).astype(BF16)
        kall[there, :] = rotated(part[:, 2 * HD : 3 * HD], cosine, sine).astype(BF16)
        vall[there, :] = part[:, 3 * HD : 4 * HD].astype(BF16)

    entered = []

    def entries(h):
        for b in range(8):
            first = pl.multiple_of(owner_of(b) * (BATCHES * SIZE) + SIZE * h, SIZE)
            here = pl.ds(stored + part_rows * h + SIZE * b, SIZE)
            pent_ref[0, pl.ds(first, SIZE), :] = kall[here, :]
            pent_ref[1, pl.ds(first, SIZE), :] = vall[here, :]
        entered.append(h)
        if len(entered) == BATCHES:
            hand(pent_ref, pent_hbm)

    def attend(h):
        rows = part_rows
        query = qb[h].reshape(2 * rows, HD)
        scores = lax.dot_general(query, kall[...], NT, preferred_element_type=F32)
        r = lax.broadcasted_iota(jnp.int32, (2 * rows, 1), 0)
        q_place = place_of(rows * h + r % rows)
        k_place = kplace[...]
        scores = jnp.where(k_place <= q_place, scores, NEGATIVE)
        top = jnp.max(scores, axis=-1, keepdims=True)
        weights = jnp.exp2((scores - top) * scale2)
        total = jnp.sum(weights, axis=-1, keepdims=True)
        result = jnp.dot(weights.astype(BF16), vall[...], preferred_element_type=F32)
        result = (result / total).astype(BF16)
        att[h, :, 0:HD] = result[:rows]
        att[h, :, HD : 2 * HD] = result[rows:]

    def out_project(h, n):
        part = jnp.dot(att[h], w_out[:, cw * n : cw * (n + 1)], preferred_element_type=F32)
        rs_split(0, h, n, part)

    def middle(h):
        mine = pl.ds(SIZE * h, SIZE)
        pieces = []
        for n in range(CHUNKS):
            cols = slice(cw * n, cw * (n + 1))
            value = (rows_ref[mine, cols].astype(F32) + rs_total(0, h, n)).astype(BF16)
            resid[mine, cols] = value
            pieces.append(value.astype(F32))
        values = jnp.concatenate(pieces, axis=1)
        xg2[h, 0:SIZE, :] = normed(values, fgain_ref[...])
        ag_start(1, h)

    steps = units // 512

    def gated(h, begin=0, end=steps):
        count = 8 * SIZE + (slots if h == JOINED else 0)
        step = 512

        def one(j, carry):
            cols = pl.ds(pl.multiple_of(j * step, step), step)
            inner = xg2[h, 0:count, :]
            gate_part = jnp.dot(inner, w_gate[:, cols], preferred_element_type=F32)
            up_part = jnp.dot(inner, w_up[:, cols], preferred_element_type=F32)
            hid[0:count, cols] = (
                gate_part / (1.0 + jnp.exp(-gate_part)) * up_part
            ).astype(BF16)
            return carry

        lax.fori_loop(begin, end, one, 0)

    def lower(h, n):
        count = 8 * SIZE + (slots if h == JOINED else 0)
        cols = slice(cw * n, cw * (n + 1))
        part = jnp.dot(hid[0:count, :], w_down[:, cols], preferred_element_type=F32)
        rs_split(1, h, n, part)
        if h == JOINED:
            dpart[2, :, cols] = part[8 * SIZE :].astype(BF16)

    def last(h):
        mine = pl.ds(SIZE * h, SIZE)
        for n in range(CHUNKS):
            cols = slice(cw * n, cw * (n + 1))
            pout_ref[mine, cols] = (resid[mine, cols].astype(F32) + rs_total(1, h, n)).astype(BF16)
        hand(pout_ref.at[mine], pout_hbm.at[mine])

    wide = 16 * slots

    def marker(head, flip):
        shape = (slots, wide) if flip else (wide, slots)
        row = lax.broadcasted_iota(jnp.int32, shape, 1 if flip else 0)
        slot = lax.broadcasted_iota(jnp.int32, shape, 0 if flip else 1)
        return (row == 16 * slot + head).astype(F32).astype(BF16)

    def decode_project():
        inner = normed(dag[0].astype(F32), again_ref[...])
        part = jnp.dot(inner, w_qkv[...], preferred_element_type=F32)
        cosine = cos_ref[fresh : fresh + slots, :]
        sine = sin_ref[fresh : fresh + slots, :]
        spread = jnp.zeros((wide, HD), F32)
        for head in range(2):
            query = rotated(part[:, HD * head : HD * (head + 1)], cosine, sine).astype(BF16)
            spread = spread + jnp.dot(marker(head, False), query, preferred_element_type=F32)
        qpad[...] = spread.astype(BF16)
        key = rotated(part[:, 2 * HD : 3 * HD], cosine, sine).astype(BF16)
        value = part[:, 3 * HD : 4 * HD].astype(BF16)
        dent_ref[0] = key
        dent_ref[1] = value
        hand(dent_ref, dent_hbm)
        knew[...] = jnp.zeros_like(knew)
        vnew[...] = jnp.zeros_like(vnew)
        knew[0:slots, :] = key
        vnew[0:slots, :] = value

    def decode_attend(begin, end):
        def score(n, carry):
            here = pl.ds(pl.multiple_of(16 * n, 16), 16)
            part = lax.dot_general(qpad[here, :], kdec[n], NT, preferred_element_type=F32)
            col = lax.broadcasted_iota(jnp.int32, (16, dstored), 1)
            dsc[here, 0:dstored] = jnp.where(col < len_ref[n], part, NEGATIVE)
            return carry

        lax.fori_loop(begin, end, score, 0, unroll=4)

    def decode_weigh():
        own = lax.dot_general(qpad[...], knew[...], NT, preferred_element_type=F32)
        row = lax.broadcasted_iota(jnp.int32, (wide, HD), 0)
        col = lax.broadcasted_iota(jnp.int32, (wide, HD), 1)
        dsc[:, dstored:] = jnp.where(col == (row >> 4), own, NEGATIVE)
        scores = dsc[...]
        top = jnp.max(scores, axis=-1, keepdims=True)
        weights = jnp.exp2((scores - top) * scale2)
        dtotal[...] = jnp.sum(weights, axis=-1, keepdims=True)
        dpr[...] = weights.astype(BF16)

    def decode_mix(begin, end):
        def mix(n, carry):
            here = pl.ds(pl.multiple_of(16 * n, 16), 16)
            dob[here, :] = jnp.dot(dpr[here, 0:dstored], vdec[n], preferred_element_type=F32)
            return carry

        lax.fori_loop(begin, end, mix, 0, unroll=4)
    def decode_finish():
        result = dob[...] + jnp.dot(dpr[:, dstored:], vnew[...], preferred_element_type=F32)
        result = (result / dtotal[...]).astype(BF16)
        picked = [
            jnp.dot(marker(head, True), result, preferred_element_type=F32).astype(BF16)
            for head in range(2)
        ]
        attended = jnp.concatenate(picked, axis=1)
        dpart[1] = jnp.dot(attended, w_out[...], preferred_element_type=F32).astype(BF16)

    def own_rows(h):
        mine = pl.ds(SIZE * h, SIZE)
        xg1[h, 0:SIZE, :] = normed(rows_ref[mine, :].astype(F32), again_ref[...])

    spot = lax.broadcasted_iota(jnp.int32, (slots, width), 0)

    def own_decode_rows():
        pair = drows_ref[...].astype(F32)
        dpart[0] = (
            jnp.where(spot == 2 * t, pair[0:1], 0.0) + jnp.where(spot == 2 * t + 1, pair[1:2], 0.0)
        ).astype(BF16)

    def tables():
        lane = lax.broadcasted_iota(jnp.int32, (1, HD), 1)
        powers = (lane % (HD // 2)).astype(F32) * (2.0 / HD)
        inverse = jnp.exp(powers * (-math.log(THETA)))
        sign = jnp.where(lane < HD // 2, -1.0, 1.0).astype(F32)

        def table(first, count, places):
            angles = places.astype(F32) * inverse
            cos_ref[pl.ds(first, count), :] = jnp.cos(angles)
            sin_ref[pl.ds(first, count), :] = jnp.sin(angles) * sign

        def some(i, carry):
            row = lax.broadcasted_iota(jnp.int32, (64, HD), 0)
            table(pl.multiple_of(64 * i, 64), 64, off_ref[0] + place_of(64 * i + row))
            return carry

        lax.fori_loop(0, fresh // 64, some, 0)
        col = lax.broadcasted_iota(jnp.int32, (1, stored + fresh), 1)
        kplace[...] = jnp.where(
            col < stored,
            jnp.where(col < off_ref[0], -1, fresh),
            place_of(jnp.maximum(col - stored, 0)),
        )
        slot = lax.broadcasted_iota(jnp.int32, (slots, HD), 0)
        length = jnp.zeros((slots, HD), jnp.int32)
        for n in range(slots):
            length = jnp.where(slot == n, len_ref[n], length)
        table(fresh, slots, length)

    member = lax.broadcasted_iota(jnp.int32, (slots, nreq), 0) + slots * g
    listed = lax.broadcasted_iota(jnp.int32, (slots, nreq), 1)

    def choices():
        request = lax.broadcasted_iota(jnp.int32, (nreq, nreq), 0)
        holder = (request == deal_ref[...]).astype(F32).astype(BF16)
        picker[...] = lax.dot_general(
            (member == listed).astype(F32).astype(BF16), holder, NT, preferred_element_type=F32
        ).astype(BF16)
        chooser[...] = (member == deal_ref[...]).astype(F32).astype(BF16)

    def first_deal():
        if across:
            pl.semaphore_wait(passed, len(across))
        dp_start(0, cr_total(0).astype(BF16))

    def dealt():
        ca_start(0, jnp.dot(chooser[...], dp_total(0), preferred_element_type=F32).astype(BF16))

    def decode_middle():
        total = dag[0, :, columns(t)].astype(F32) + cr_total(1)
        ca_start(1, total.astype(BF16))

    def decode_inner():
        ca_finish(1)
        xg2[JOINED, part_rows:, :] = normed(dag[1].astype(F32), fgain_ref[...])

    def decode_last():
        total = dag[1, :, columns(t)].astype(F32) + cr_total(2)
        dp_start(1, total.astype(BF16))

    def undealt():
        ca_start(2, jnp.dot(picker[...], dp_total(1), preferred_element_type=F32).astype(BF16))

    def decode_out():
        ca_finish(2)
        every = dag[2].astype(F32)
        first = jnp.sum(jnp.where(spot == 2 * t, every, 0.0), axis=0, keepdims=True)
        second = jnp.sum(jnp.where(spot == 2 * t + 1, every, 0.0), axis=0, keepdims=True)
        dout_ref[...] = jnp.concatenate([first, second], axis=0).astype(BF16)
        hand(dout_ref, dout_hbm)

    for name in ("rows", "drows", "again", "off", "len", "deal", "fgain"):
        local[name].wait()
    own_decode_rows()
    own_rows(0)
    own_rows(1)

    pl.semaphore_wait(barrier, 7 + len(below) + len(across))
    for other in across:
        pl.semaphore_signal(passed, inc=1, device_id=(other, t), device_id_type=MESH)


    cr_start(0)
    ag_start(0, 0)
    ag_start(0, 1)
    own_rows(2)
    ag_start(0, 2)
    own_rows(3)
    ag_start(0, 3)
    tables()
    choices()
    ag_onward(0, 0)
    first_deal()
    ag_share(0, 0)
    ag_onward(0, 1)
    ag_share(0, 1)
    ag_onward(0, 2)
    ag_share(0, 2)
    ag_onward(0, 3)
    ag_share(0, 3)
    ag_far(0, 0)
    ag_far(0, 1)
    dealt()
    local["qkv"].wait()
    ag_finish(0, 0)
    project(0)
    ag_far(0, 2)
    entries(0)
    ag_finish(0, 1)
    project(1)
    ag_far(0, 3)
    entries(1)
    ag_finish(0, 2)
    project(2)
    entries(2)
    ag_finish(0, 3)
    project(3)
    local["pk"].wait()
    local["pv"].wait()
    local["out"].wait()
    attend(0)
    out_project(0, 0)
    out_project(0, 1)
    attend(1)
    out_project(1, 0)
    out_project(1, 1)
    entries(3)
    rs_combine(0, 0)
    attend(2)
    out_project(2, 0)
    ca_finish(0)
    decode_project()
    rs_combine(0, 1)
    local["dk"].wait()
    decode_attend(0, slots // 2)
    out_project(2, 1)
    attend(3)
    rs_relay(0, 0)
    out_project(3, 0)
    out_project(3, 1)
    rs_combine(0, 2)
    decode_attend(slots // 2, slots)
    decode_weigh()
    rs_relay(0, 1)
    local["dv"].wait()
    decode_mix(0, slots // 2)
    rs_combine(0, 3)
    decode_mix(slots // 2, slots)
    decode_finish()
    cr_start(1)
    middle(0)
    rs_relay(0, 2)
    middle(1)
    rs_relay(0, 3)
    ag_onward(1, 0)
    decode_middle()
    ag_share(1, 0)
    middle(2)
    ag_onward(1, 1)
    ag_share(1, 1)
    middle(3)
    ag_far(1, 0)
    ag_onward(1, 2)
    decode_inner()
    local["gate"].wait()
    local["up"].wait()
    local["down"].wait()
    ag_finish(1, 0)
    gated(0, 0, steps // 2)
    gated(0, steps // 2, steps)
    ag_far(1, 1)
    lower(0, 0)
    ag_onward(1, 3)
    ag_share(1, 2)
    lower(0, 1)
    cr_start(2)
    ag_share(1, 3)
    ag_finish(1, 1)
    gated(1, 0, steps // 2)
    ag_far(1, 2)
    gated(1, steps // 2, steps)
    rs_combine(1, 0)
    lower(1, 0)
    lower(1, 1)
    ag_finish(1, 2)
    gated(2, 0, steps // 2)
    ag_far(1, 3)
    gated(2, steps // 2, steps)
    lower(2, 0)
    rs_combine(1, 1)
    decode_last()
    lower(2, 1)
    ag_finish(1, 3)
    gated(3, 0, steps // 2)
    rs_relay(1, 0)
    gated(3, steps // 2, steps)
    rs_combine(1, 2)
    lower(3, 0)
    lower(3, 1)
    rs_relay(1, 1)
    rs_combine(1, 3)
    last(0)
    rs_relay(1, 2)
    undealt()
    last(1)
    rs_relay(1, 3)
    last(2)
    decode_out()
    last(3)

    for copy in sends:
        copy.wait_send()
    for copy in handed:
        copy.wait()


def hand_out(*refs):
    count = len(refs) // 3 + 1
    sources, targets, sems = refs[:count], refs[count : 2 * count], refs[2 * count]
    copies = [
        pltpu.make_async_copy(source, target, sems.at[i])
        for i, (source, target) in enumerate(zip(sources, targets))
    ]
    for copy in copies:
        copy.start()
    for copy in copies:
        copy.wait()


def on_device(
    groups,
    prefill_rows,
    decode_rows,
    deal_order,
    prefill_offset,
    cache_length,
    prefill_cache,
    decode_cache,
    qkv_weight,
    out_weight,
    attention_gain,
    forward_gain,
    gate_weight,
    up_weight,
    down_weight,
):
    width = prefill_rows.shape[1]
    fresh = 8 * prefill_rows.shape[0]
    slots = cache_length.shape[0]
    stored = prefill_cache.shape[2]
    dstored = decode_cache.shape[2]
    units = gate_weight.shape[1]
    cw = width // CHUNKS
    bw = width // 8
    vmem = pl.BlockSpec(memory_space=pltpu.VMEM)
    hbm = pl.BlockSpec(memory_space=pl.ANY)
    dma = pltpu.SemaphoreType.DMA
    shape = jax.ShapeDtypeStruct
    results = pl.pallas_call(
        functools.partial(layer_kernel, groups),
        name="layer",
        out_shape=(
            shape(prefill_rows.shape, BF16),
            shape(decode_rows.shape, BF16),
            shape((2, fresh, HD), BF16),
            shape((2, slots, HD), BF16),
        ),
        in_specs=[pl.BlockSpec(memory_space=pltpu.HBM)] * 7 + [hbm] * 7,
        out_specs=(hbm,) * 4,
        scratch_shapes=[
            pltpu.VMEM((width, 4 * HD), BF16),
            pltpu.VMEM((2 * HD, width), BF16),
            pltpu.VMEM((width, units), BF16),
            pltpu.VMEM((width, units), BF16),
            pltpu.VMEM((units, width), BF16),
            pltpu.VMEM((stored + fresh, HD), BF16),
            pltpu.VMEM((stored + fresh, HD), BF16),
            pltpu.VMEM((slots, dstored, HD), BF16),
            pltpu.VMEM((slots, dstored, HD), BF16),
            pltpu.VMEM((BATCHES, 8 * SIZE, width), BF16),
            pltpu.VMEM((BATCHES, 8 * SIZE + slots, width), BF16),
            pltpu.VMEM((1, stored + fresh), jnp.int32),
            pltpu.VMEM((slots, groups * slots), BF16),
            pltpu.VMEM((slots, groups * slots), BF16),
            pltpu.VMEM((16 * slots, 1), F32),
            pltpu.VMEM((BATCHES, 2, 8 * SIZE, HD), BF16),
            pltpu.VMEM((BATCHES, 8 * SIZE, 2 * HD), BF16),
            pltpu.VMEM((2, BATCHES, CHUNKS, 2, 4, SIZE, cw), BF16),
            pltpu.VMEM((2, BATCHES, CHUNKS, 4, SIZE, cw), BF16),
            pltpu.VMEM((2, BATCHES, CHUNKS, 4, SIZE, cw), BF16),
            pltpu.VMEM((2, BATCHES, CHUNKS, SIZE, cw), BF16),
            pltpu.VMEM((2, BATCHES, CHUNKS, 2, SIZE, cw), BF16),
            pltpu.VMEM(prefill_rows.shape, BF16),
            pltpu.VMEM((8 * SIZE + slots, units), BF16),
            pltpu.VMEM((3, slots, width), BF16),
            pltpu.VMEM((3, 8, slots, bw), BF16),
            pltpu.VMEM((2, groups, slots, bw), BF16),
            pltpu.VMEM((3, slots, width), BF16),
            pltpu.VMEM((16 * slots, dstored + HD), F32),
            pltpu.VMEM((16 * slots, dstored + HD), BF16),
            pltpu.VMEM((16 * slots, HD), BF16),
            pltpu.VMEM((HD, HD), BF16),
            pltpu.VMEM((HD, HD), BF16),
            pltpu.VMEM((16 * slots, HD), F32),
            pltpu.VMEM((fresh + slots, HD), F32),
            pltpu.VMEM((fresh + slots, HD), F32),
            dma((16,)),
            dma((2, BATCHES, 10)),
            dma((2, BATCHES, 10)),
            dma((2, BATCHES, CHUNKS, 4)),
            dma((2, BATCHES, CHUNKS, 4)),
            dma((3, 8)),
            dma((3, 8)),
            dma((2, groups)),
            dma((2, groups)),
            dma((3, 8)),
            dma((3, 8)),
            pltpu.SemaphoreType.REGULAR,
            pltpu.VMEM(prefill_rows.shape, BF16),
            pltpu.VMEM(decode_rows.shape, BF16),
            pltpu.VMEM((1, groups * slots), jnp.int32),
            pltpu.SMEM((1,), jnp.int32),
            pltpu.SMEM((slots,), jnp.int32),
            pltpu.VMEM((1, width), F32),
            pltpu.VMEM((1, width), F32),
            pltpu.VMEM(prefill_rows.shape, BF16),
            pltpu.VMEM(decode_rows.shape, BF16),
            pltpu.VMEM((2, fresh, HD), BF16),
            pltpu.VMEM((2, slots, HD), BF16),
            dma((8,)),
        ],
        compiler_params=pltpu.CompilerParams(
            collective_id=0, has_side_effects=True, vmem_limit_bytes=66_000_000
        ),
    )(
        prefill_rows,
        decode_rows,
        deal_order[None, :],
        prefill_offset,
        cache_length,
        attention_gain[None, :],
        forward_gain[None, :],
        prefill_cache,
        decode_cache,
        qkv_weight.reshape(width, 4 * HD),
        out_weight,
        gate_weight,
        up_weight,
        down_weight,
    )
    return pl.pallas_call(
        hand_out,
        name="hand_out",
        out_shape=tuple(shape(result.shape, BF16) for result in results),
        in_specs=[vmem] * 4,
        out_specs=(hbm,) * 4,
        scratch_shapes=[dma((4,))],
    )(*results)


def solution(mesh):
    placed = (
        P(("dp", "tensor"), None),
        P(("dp", "tensor"), None),
        P(),
        P("dp"),
        P("dp"),
        P(None, "dp", None, "tensor"),
        P(None, "dp", None, "tensor"),
        P(None, "tensor", None),
        P("tensor", None),
        P(),
        P(),
        P(None, "tensor"),
        P(None, "tensor"),
        P("tensor", None),
    )
    return jax.shard_map(
        functools.partial(on_device, mesh.shape["dp"]),
        mesh=mesh,
        in_specs=placed,
        out_specs=(
            P(("dp", "tensor"), None),
            P(("dp", "tensor"), None),
            P(None, "dp", "tensor"),
            P(None, "dp", "tensor"),
        ),
        check_vma=False,
    )
```
